32 devices in a mesh: sec: 2 (over core), section: 4 (over y, x), dp: 4 (over z).
Axes of the slice: x: 2, y: 2, z: 4, core: 2. Of those that a mesh axis runs over, the one named last changes fastest.
Arguments:
- enc_states: bfloat16 [4, 128, 4096], P('dp', None, ('sec', 'section')), may hold values from -6 to 6
- norm_gain: float32 [4096], replicated, may hold values from 0.5 to 9, as said below
- kv_weight: bfloat16 [2, 4096, 4096], P('sec', None, 'section'), may hold values from -0.09375 to 0.09375
- queries: bfloat16 [2, 4, 256, 2048], P('sec', 'dp', None, 'section'), may hold values from -6 to 6
- attn_cotangent: bfloat16 [2, 4, 256, 2048], P('sec', 'dp', None, 'section'), may hold values from -6 to 6
- target_lengths: int32 [4], P('dp'), may hold values from 64 to 256, as said below
Outputs:
- attended: bfloat16 [2, 4, 256, 2048], P('sec', 'dp', None, 'section')
- enc_grad: bfloat16 [4, 128, 4096], P('dp', None, ('sec', 'section'))
- gain_grad: float32 [4096], P(('sec', 'section', 'dp'))
- row_dot: float32 [4, 128], P('dp')
The draws below stay inside these ranges and needn't reach their ends.
Inputs may be any that keep to these rules, and one draw needn't show every extreme that they name: `target_lengths`: some sequence has all 256 tokens live. `norm_gain`: positive gains.
All inputs are finite; a program needn't handle non-finite values.
Results may differ from the reference program's by a relative error of at most 0.012.
The reference program's roundings to bfloat16 on the way (of `memory`, `weights_b`, `masked`, `score_grad` and `kv_grad`) count: a program that leaves them out, or rounds other values in their place, can miss the bound.
Values may be sent and summed in bfloat16 or wider, within the bound.
No kernel may reach another device: no remote copies, remote signals or barrier semaphores. Data moves between devices by JAX's collectives and lax.ppermute only.
A program may use at most 64 MiB of HBM per device.

```python
import jax
import jax.numpy as jnp
from jax import lax

D = 4096
HS = 256
ENC_LEN = 128
DEC_LEN = 256
HEADS = 8
LAYERS = 2
SEQS = 4


def draw_target_lengths(key, part):
    first_key, second_key = jax.random.split(jax.random.fold_in(key, 17))
    drawn = jax.random.randint(first_key, (SEQS,), DEC_LEN // 4, DEC_LEN + 1)
    chosen = jax.random.randint(second_key, (), 0, SEQS)
    return jnp.where(jnp.arange(SEQS) == chosen, DEC_LEN, drawn).astype(jnp.int32)


def draw_norm_gain(key, part):
    gain_key = jax.random.fold_in(key, 29)
    position = jnp.arange(D).astype(jnp.float32) / (D - 1)
    factor = jax.random.uniform(gain_key, (D,), jnp.float32, 0.7, 1.3)
    return (jnp.exp(jnp.log(4.0) * position) * factor).astype(jnp.float32)


def with_spikes(entries, key, source, target, shards_of, factor):
    def block_of(dim):
        return (jnp.arange(entries.shape[dim]) // (entries.shape[dim] // shards_of)).reshape((-1,) + (1,) * (entries.ndim - 1 - dim))

    first = jax.random.permutation(key, shards_of)[block_of(target)]
    other_side = (block_of(target) + shards_of // 2) % shards_of
    return jnp.where((block_of(source) == first) | (block_of(source) == other_side), factor * entries, entries)


def level_of(rng, shape, pieces, low, largest):
    factor_of, own = 1.0, jax.random.fold_in(rng, 6)
    for dim, blocks in pieces:
        heights = jnp.exp(jax.random.uniform(jax.random.fold_in(own, dim), (blocks,), jnp.float32, low / len(pieces), largest / len(pieces)))
        factor_of = factor_of * jnp.repeat(heights, shape[dim] // blocks).reshape([-1 if axis == dim else 1 for axis in range(len(shape))])
    return factor_of


def bell_draw(key, extent, spread, reach, pieces=(), kind=jnp.bfloat16):
    values = jax.random.normal(key, extent, jnp.float32) * spread
    if len(pieces) > 0:
        values = level_of(key, extent, pieces, -0.22, 0.18) * values
    return jnp.clip(values, min=-reach, max=reach).astype(kind)


def noise_with(rng, dims, width, most, cuts, heavy, held_as=jnp.bfloat16):
    array = width * jax.random.normal(rng, dims, jnp.float32)
    if cuts:
        array = array * level_of(rng, dims, cuts, -0.22, 0.18)
    return jnp.clip(with_spikes(array, jax.random.fold_in(rng, 3), *heavy), -most, most).astype(held_as)


def setup_inputs(seed: int = 0) -> dict:
    seeds = jax.random.split(jax.random.key(seed), 7)
    enc_states = noise_with(seeds[0], (SEQS, ENC_LEN, D), 1.0, 6.0, ((0, 4), (2, 8)), (0, 2, 4, 2.0))
    norm_gain = draw_norm_gain(jax.random.fold_in(seeds[6], 71), 0)
    kv_weight = bell_draw(seeds[2], (LAYERS, D, 2 * HEADS * HS), D ** -0.5, 0.09375, ((0, 2), (2, 4)))
    queries = bell_draw(seeds[3], (LAYERS, SEQS, DEC_LEN, HEADS * HS), 1.0, 6.0, ((0, 2), (1, 4), (3, 4)))
    attn_cotangent = bell_draw(seeds[4], (LAYERS, SEQS, DEC_LEN, HEADS * HS), 1.0, 6.0, ((0, 2), (1, 4), (3, 4)))
    target_lengths = draw_target_lengths(jax.random.fold_in(seeds[6], 71), 0)
    return dict(enc_states=enc_states, norm_gain=norm_gain, kv_weight=kv_weight, queries=queries, attn_cotangent=attn_cotangent, target_lengths=target_lengths)


def reference(enc_states, norm_gain, kv_weight, queries, attn_cotangent, target_lengths):
    score_scale = HS ** (-0.5)
    head_count = queries.shape[-1] // HS

    def per_sequence(inputs):
        enc_rows, query_all, cot_all, length = inputs
        rows = enc_rows.astype(jnp.float32)
        inv_rms = lax.rsqrt(lax.optimization_barrier(jnp.mean(rows * rows, axis=-1)) + 1e-06)
        normed = rows * inv_rms[:, None]
        memory = (normed * norm_gain).astype(jnp.bfloat16)
        live_rows = jnp.arange(DEC_LEN) < length

        def per_layer(carry, layer_in):
            weight, query_flat, cot_flat = layer_in
            key_value = jnp.dot(memory, weight, preferred_element_type=jnp.float32)
            key_value = key_value.reshape(ENC_LEN, head_count, 2, HS)
            key_rows = key_value[:, :, 0].astype(jnp.bfloat16).astype(jnp.float32)
            value_rows = key_value[:, :, 1].astype(jnp.bfloat16).astype(jnp.float32)
            query_rows = query_flat.reshape(DEC_LEN, head_count, HS).astype(jnp.float32)
            cot_rows = cot_flat.reshape(DEC_LEN, head_count, HS)
            scores = jnp.einsum('thd,shd->hts', query_rows, key_rows) * score_scale
            exponent = jnp.exp(scores)
            attention = exponent / lax.optimization_barrier(jnp.sum(exponent, axis=-1, keepdims=True))
            weights_b = attention.astype(jnp.bfloat16).astype(jnp.float32)
            attended = jnp.einsum('hts,shd->thd', weights_b, value_rows).astype(jnp.bfloat16)
            masked = jnp.where(live_rows[:, None, None], cot_rows, jnp.zeros_like(cot_rows)).astype(jnp.float32)
            back_prod = jnp.einsum('thd,shd->hts', masked, value_rows)
            score_grad = attention * (back_prod - lax.optimization_barrier(jnp.sum(attention * back_prod, axis=-1, keepdims=True))) * score_scale
            score_grad = score_grad.astype(jnp.bfloat16).astype(jnp.float32)
            key_grad = jnp.einsum('hts,thd->shd', score_grad, query_rows)
            value_grad = jnp.einsum('hts,thd->shd', weights_b, masked)
            kv_grad = jnp.stack([key_grad, value_grad], axis=2).reshape(ENC_LEN, 2 * head_count * HS).astype(jnp.bfloat16)
            carry = carry + jnp.dot(kv_grad, weight.T, preferred_element_type=jnp.float32)
            return (carry, attended.reshape(DEC_LEN, head_count * HS))
        start_grad = jnp.zeros((ENC_LEN, D), jnp.float32)
        memory_grad, attended = lax.scan(per_layer, start_grad, (kv_weight, query_all, cot_all))
        gain_scaled = memory_grad * norm_gain
        row_dot = lax.optimization_barrier(jnp.sum(gain_scaled * normed, axis=-1))
        enc_grad = (inv_rms[:, None] * (gain_scaled - normed * row_dot[:, None] / D)).astype(jnp.bfloat16)
        gain_term = lax.optimization_barrier(jnp.sum(memory_grad * normed, axis=0))
        return (attended, enc_grad, gain_term, row_dot)
    query_seq = jnp.transpose(queries, (1, 0, 2, 3))
    cot_seq = jnp.transpose(attn_cotangent, (1, 0, 2, 3))
    attended, enc_grad, gain_terms, row_dot = lax.map(per_sequence, (enc_states, query_seq, cot_seq, target_lengths))
    attended = jnp.transpose(attended, (1, 0, 2, 3))
    gain_grad = lax.optimization_barrier(jnp.sum(gain_terms, axis=0))
    return (attended, enc_grad, gain_grad, row_dot)
```

```python
import functools

import jax
import jax.numpy as jnp
from jax import lax
from jax.experimental import pallas as pl
from jax.experimental.pallas import tpu as pltpu
from jax.sharding import PartitionSpec as P

HS = 256
EPS = 1e-06
LAST = (((1,), (1,)), ((), ()))
FIRST = (((0,), (0,)), ((), ()))
VMEM = pl.BlockSpec(memory_space=pltpu.VMEM)
SMEM = pl.BlockSpec(memory_space=pltpu.SMEM)
ANY = pl.BlockSpec(memory_space=pl.ANY)


def partner(index, step, count):
    return index ^ step


def tree_sum(terms):
    while len(terms) > 1:
        terms = [terms[i] + terms[i + 1] for i in range(0, len(terms), 2)]
    return terms[0]


def main_kernel(
    parts,
    heads,
    where_ref,
    length_ref,
    *refs,
):
    chunk_refs = refs[: 2 * parts]
    (gain_ref, weight_hbm, query_ref, cot_ref) = refs[2 * parts : 2 * parts + 4]
    (att_ref, sib_ref, own_ref, inv_ref, row_ref) = refs[2 * parts + 4 : 2 * parts + 9]
    (weight, memory, kv, kv_grad, sems) = refs[2 * parts + 9 :]
    tokens, feats = chunk_refs[0].shape
    width = weight.shape[0]
    half = width // 2
    blocks = sems.shape[0]
    block = width // blocks

    copies = []
    for b in range(blocks):
        rows = pl.ds(b * block, block)
        copy = pltpu.make_async_copy(weight_hbm.at[rows], weight.at[rows], sems.at[b])
        copy.start()
        copies.append(copy)

    square = None
    for ref in chunk_refs:
        x = ref[...].astype(jnp.float32)
        part = jnp.sum(x * x, axis=1, keepdims=True)
        square = part if square is None else square + part
    inv_rms = lax.rsqrt(square / width + EPS)
    inv_ref[...] = inv_rms
    for j, ref in enumerate(chunk_refs):
        at = pl.multiple_of(where_ref[j] * feats, feats)
        normed = ref[...].astype(jnp.float32) * inv_rms
        memory[:, pl.ds(at, feats)] = (normed * gain_ref[:, pl.ds(at, feats)]).astype(jnp.bfloat16)

    for b in range(blocks):
        copies[b].wait()
        rows = pl.ds(b * block, block)
        product = jnp.dot(memory[:, rows], weight[rows, :], preferred_element_type=jnp.float32)
        if b == 0:
            kv[...] = product
        else:
            kv[...] += product

    scale = HS ** (-0.5)
    live = lax.broadcasted_iota(jnp.int32, (query_ref.shape[0], HS), 0) < length_ref[0]
    row_part = None
    for h in range(heads):
        cols = pl.ds(h * HS, HS)
        key_cols, value_cols = pl.ds(2 * h * HS, HS), pl.ds((2 * h + 1) * HS, HS)
        key_full, value_full = kv[:, key_cols], kv[:, value_cols]
        key_rows, value_rows = key_full.astype(jnp.bfloat16), value_full.astype(jnp.bfloat16)
        query = query_ref[:, cols]
        cot = cot_ref[:, cols]
        masked = jnp.where(live, cot, jnp.zeros_like(cot))
        scores = lax.dot_general(key_rows, query, LAST, preferred_element_type=jnp.float32) * scale
        exponent = jnp.exp(scores)
        attention = exponent * (1.0 / jnp.sum(exponent, axis=0, keepdims=True))
        weights_b = attention.astype(jnp.bfloat16)
        att_ref[:, cols] = lax.dot_general(
            weights_b, value_rows, FIRST, preferred_element_type=jnp.float32
        ).astype(jnp.bfloat16)
        back = lax.dot_general(value_rows, masked, LAST, preferred_element_type=jnp.float32)
        mean = jnp.sum(attention * back, axis=0, keepdims=True)
        score_grad = (attention * (back - mean) * scale).astype(jnp.bfloat16)
        key_grad = jnp.dot(score_grad, query, preferred_element_type=jnp.float32)
        value_grad = jnp.dot(weights_b, masked, preferred_element_type=jnp.float32)
        key_grad, value_grad = key_grad.astype(jnp.bfloat16), value_grad.astype(jnp.bfloat16)
        kv_grad[:, key_cols] = key_grad
        kv_grad[:, value_cols] = value_grad
        here = jnp.sum(
            key_grad.astype(jnp.float32) * key_full + value_grad.astype(jnp.float32) * value_full,
            axis=1,
            keepdims=True,
        )
        row_part = here if row_part is None else row_part + here
    row_ref[...] = jnp.transpose(jnp.broadcast_to(row_part, (tokens, 128)))[0:1, :]

    me = where_ref[2 * parts]
    grad = kv_grad[...]
    tile = half // 4
    for t in range(4):
        rows = pl.ds(pl.multiple_of((1 - me) * half + t * tile, tile), tile)
        sib_ref[:, pl.ds(t * tile, tile)] = lax.dot_general(
            grad, weight[rows, :], LAST, preferred_element_type=jnp.float32
        ).astype(jnp.bfloat16)
    for t in range(4):
        rows = pl.ds(pl.multiple_of(me * half + t * tile, tile), tile)
        own_ref[:, pl.ds(t * tile, tile)] = lax.dot_general(
            grad, weight[rows, :], LAST, preferred_element_type=jnp.float32
        )


def chip_kernel(parts, where_ref, own_ref, sib_ref, row_ref, row_sib_ref, inv_ref, *refs):
    chunk_refs = refs[:parts]
    kept_ref = refs[parts]
    big_refs = refs[parts + 1 : 2 * parts]
    small_refs = refs[2 * parts :]
    feats = chunk_refs[0].shape[1]
    inv_rms = inv_ref[...]
    row = row_ref[...] + row_sib_ref[...]
    for k in range(parts):
        at = pl.multiple_of(where_ref[k] * feats, feats)
        cols = pl.ds(at, feats)
        total = own_ref[:, cols] + sib_ref[:, cols].astype(jnp.float32)
        if k == 0:
            kept_ref[...] = total
        else:
            big_refs[k - 1][...] = total.astype(jnp.bfloat16)
        normed = chunk_refs[k][...].astype(jnp.float32) * inv_rms
        small_refs[k][:, pl.ds(0, feats)] = jnp.sum(total * normed, axis=0, keepdims=True)
        small_refs[k][:, pl.ds(feats, row.shape[1])] = row


def last_kernel(parts, width, where_ref, kept_ref, *refs):
    big_refs = refs[: parts - 1]
    chunk_ref, inv_ref, gain_ref, row_ref, enc_ref = refs[parts - 1 :]
    tokens, feats = chunk_ref.shape
    grad = kept_ref[...]
    for ref in big_refs:
        grad = grad + ref[...].astype(jnp.float32)
    inv_rms = inv_ref[...]
    at = pl.multiple_of(where_ref[0] * feats, feats)
    gain = gain_ref[:, pl.ds(at, feats)]
    normed = chunk_ref[...].astype(jnp.float32) * inv_rms
    row_dot = jnp.transpose(jnp.broadcast_to(row_ref[...], (128, tokens)))[:, 0:1]
    enc_ref[...] = (inv_rms * (gain * grad - normed * (row_dot / width))).astype(jnp.bfloat16)


def per_device(sizes, enc_states, norm_gain, kv_weight, queries, attn_cotangent, target_lengths):
    cores, parts, seqs = sizes
    rows = enc_states[0]
    tokens, feats = rows.shape
    weight = kv_weight[0]
    width = weight.shape[0]
    half = width // 2
    query, cot = queries[0, 0], attn_cotangent[0, 0]
    dec = query.shape[0]
    heads = query.shape[1] // HS
    gain = norm_gain.reshape(1, width)
    core = lax.axis_index("sec")
    section = lax.axis_index("section")
    swap = [(0, 1), (1, 0)]

    def to_section(x, step):
        return lax.ppermute(x, "section", [(i, partner(i, step, parts)) for i in range(parts)])

    def to_core(x):
        return lax.ppermute(x, "sec", swap)

    chunks = [rows] + [to_section(rows, k) for k in range(1, parts)]
    others = [to_core(c) for c in chunks]
    peers = [partner(section, k, parts) for k in range(parts)]
    where = jnp.stack(
        [core * parts + p for p in peers] + [(1 - core) * parts + p for p in peers] + [core]
    ).astype(jnp.int32)

    blocks = 8
    flops = 2 * tokens * width * weight.shape[1]
    att, sib, own, inv_rms, row = pl.pallas_call(
        functools.partial(main_kernel, parts, heads),
        out_shape=(
            jax.ShapeDtypeStruct(query.shape, jnp.bfloat16),
            jax.ShapeDtypeStruct((tokens, half), jnp.bfloat16),
            jax.ShapeDtypeStruct((tokens, half), jnp.float32),
            jax.ShapeDtypeStruct((tokens, 1), jnp.float32),
            jax.ShapeDtypeStruct((1, tokens), jnp.float32),
        ),
        in_specs=[SMEM, SMEM] + [VMEM] * (2 * parts) + [VMEM, ANY, VMEM, VMEM],
        out_specs=(VMEM,) * 5,
        scratch_shapes=[
            pltpu.VMEM(weight.shape, jnp.bfloat16),
            pltpu.VMEM((tokens, width), jnp.bfloat16),
            pltpu.VMEM((tokens, weight.shape[1]), jnp.float32),
            pltpu.VMEM((tokens, weight.shape[1]), jnp.bfloat16),
            pltpu.SemaphoreType.DMA((blocks,)),
        ],
        compiler_params=pltpu.CompilerParams(vmem_limit_bytes=40 << 20),
        cost_estimate=pl.CostEstimate(
            flops=3 * flops, bytes_accessed=2 * weight.size, transcendentals=dec * tokens * heads
        ),
        name="main",
    )(where, target_lengths, *chunks, *others, gain, weight, query, cot)

    row_sib = to_core(row)
    sib_in = to_core(sib)

    where_section = jnp.stack(peers).astype(jnp.int32)
    pieces = pl.pallas_call(
        functools.partial(chip_kernel, parts),
        out_shape=(jax.ShapeDtypeStruct((tokens, feats), jnp.float32),)
        + (jax.ShapeDtypeStruct((tokens, feats), jnp.bfloat16),) * (parts - 1)
        + (jax.ShapeDtypeStruct((1, feats + tokens), jnp.float32),) * parts,
        in_specs=[SMEM] + [VMEM] * (5 + parts),
        out_specs=(VMEM,) * (2 * parts),
        compiler_params=pltpu.CompilerParams(vmem_limit_bytes=16 << 20),
        cost_estimate=pl.CostEstimate(
            flops=4 * tokens * half, bytes_accessed=8 * tokens * half, transcendentals=0
        ),
        name="chip",
    )(where_section, own, sib_in, row, row_sib, inv_rms, *chunks)
    kept, big, small = pieces[0], pieces[1:parts], pieces[parts:]

    small_in = [small[0]] + [to_section(small[k], k) for k in range(1, parts)]
    big_in = [to_section(big[k - 1], k) for k in range(1, parts)]
    sums = tree_sum(small_in)
    gain_term = sums[0, :feats]
    row_dot = sums[:, feats:]
    piece = feats // seqs
    if seqs <= 8:
        dp = lax.axis_index("dp")
        owned = [
            lax.dynamic_slice_in_dim(gain_term, partner(dp, k, seqs) * piece, piece, 0)
            for k in range(seqs)
        ]
        gain_grad = tree_sum(
            [owned[0]]
            + [
                lax.ppermute(owned[k], "dp", [(i, partner(i, k, seqs)) for i in range(seqs)])
                for k in range(1, seqs)
            ]
        )
    else:
        gain_grad = lax.psum_scatter(gain_term, "dp", scatter_dimension=0, tiled=True)

    where_own = (core * parts + section).reshape(1).astype(jnp.int32)
    enc_grad = pl.pallas_call(
        functools.partial(last_kernel, parts, width),
        out_shape=jax.ShapeDtypeStruct((tokens, feats), jnp.bfloat16),
        in_specs=[SMEM] + [VMEM] * (4 + parts),
        out_specs=VMEM,
        compiler_params=pltpu.CompilerParams(vmem_limit_bytes=8 << 20),
        cost_estimate=pl.CostEstimate(
            flops=10 * tokens * feats, bytes_accessed=16 * tokens * feats, transcendentals=0
        ),
        name="last",
    )(where_own, kept, *big_in, rows, inv_rms, gain, row_dot)
    return (att[None, None], enc_grad[None], gain_grad, row_dot)


def solution(mesh):
    sizes = tuple(mesh.shape[a] for a in ("sec", "section", "dp"))
    placed = (
        P("dp", None, ("sec", "section")),
        P(),
        P("sec", None, "section"),
        P("sec", "dp", None, "section"),
        P("sec", "dp", None, "section"),
        P("dp"),
    )
    return jax.shard_map(
        functools.partial(per_device, sizes),
        mesh=mesh,
        in_specs=placed,
        out_specs=(
            P("sec", "dp", None, "section"),
            P("dp", None, ("sec", "section")),
            P(("sec", "section", "dp")),
            P("dp", None),
        ),
        check_vma=False,
    )
```

```python
import functools

import jax
import jax.numpy as jnp
from jax import lax
from jax.experimental import pallas as pl
from jax.experimental.pallas import tpu as pltpu
from jax.sharding import PartitionSpec as P

HS = 256
EPS = 1e-06
LAST = (((1,), (1,)), ((), ()))
FIRST = (((0,), (0,)), ((), ()))
VMEM = pl.BlockSpec(memory_space=pltpu.VMEM)
SMEM = pl.BlockSpec(memory_space=pltpu.SMEM)
ANY = pl.BlockSpec(memory_space=pl.ANY)


def partner(index, step, count):
    return index ^ step


def tree_sum(terms):
    while len(terms) > 1:
        terms = [terms[i] + terms[i + 1] for i in range(0, len(terms), 2)]
    return terms[0]


def direct_sum(terms, axis, count):
    perms = [[(i, partner(i, k, count)) for i in range(count)] for k in range(count)]
    return tree_sum([terms[0]] + [lax.ppermute(terms[k], axis, perms[k]) for k in range(1, count)])


def first_kernel(rows_ref, weight_ref, square_ref):
    own = rows_ref[...].astype(jnp.float32)
    square_ref[...] = jnp.sum(own * own, axis=1, keepdims=True)


def main_kernel(
    parts,
    heads,
    length_ref,
    square_ref,
    *refs,
):
    chunk_refs = refs[: 2 * parts]
    (gain_ref, weight, query_ref, cot_ref) = refs[2 * parts : 2 * parts + 4]
    (att_ref, sib_ref, own_ref, inv_ref, row_ref) = refs[2 * parts + 4 : 2 * parts + 9]
    (memory, kv, kv_grad) = refs[2 * parts + 9 :]
    tokens, feats = chunk_refs[0].shape
    width = weight.shape[0]
    half = width // 2

    square = square_ref[...]
    for ref in chunk_refs[1:]:
        x = ref[...].astype(jnp.float32)
        part = jnp.sum(x * x, axis=1, keepdims=True)
        square = square + part
    inv_rms = lax.rsqrt(square / width + EPS)
    inv_ref[...] = inv_rms
    me, section = lax.axis_index("sec"), lax.axis_index("section")
    for j, ref in enumerate(chunk_refs):
        owner = me if j < parts else 1 - me
        at = pl.multiple_of((owner * parts + partner(section, j % parts, parts)) * feats, feats)
        normed = ref[...].astype(jnp.float32) * inv_rms
        memory[:, pl.ds(at, feats)] = (normed * gain_ref[:, pl.ds(at, feats)]).astype(jnp.bfloat16)

    kv[...] = jnp.dot(memory[...], weight[...], preferred_element_type=jnp.float32)

    scale = HS ** (-0.5)
    live = lax.broadcasted_iota(jnp.int32, (query_ref.shape[0], HS), 0) < length_ref[0]
    row_part = None
    for h in range(heads):
        cols = pl.ds(h * HS, HS)
        key_cols, value_cols = pl.ds(2 * h * HS, HS), pl.ds((2 * h + 1) * HS, HS)
        key_full, value_full = kv[:, key_cols], kv[:, value_cols]
        key_rows, value_rows = key_full.astype(jnp.bfloat16), value_full.astype(jnp.bfloat16)
        query = query_ref[:, cols]
        cot = cot_ref[:, cols]
        masked = jnp.where(live, cot, jnp.zeros_like(cot))
        scores = lax.dot_general(key_rows, query, LAST, preferred_element_type=jnp.float32) * scale
        exponent = jnp.exp(scores)
        attention = exponent * (1.0 / jnp.sum(exponent, axis=0, keepdims=True))
        weights_b = attention.astype(jnp.bfloat16)
        att_ref[:, cols] = lax.dot_general(
            weights_b, value_rows, FIRST, preferred_element_type=jnp.float32
        ).astype(jnp.bfloat16)
        back = lax.dot_general(value_rows, masked, LAST, preferred_element_type=jnp.float32)
        mean = jnp.sum(attention * back, axis=0, keepdims=True)
        score_grad = (attention * (back - mean) * scale).astype(jnp.bfloat16)
        key_grad = jnp.dot(score_grad, query, preferred_element_type=jnp.float32)
        value_grad = jnp.dot(weights_b, masked, preferred_element_type=jnp.float32)
        key_grad, value_grad = key_grad.astype(jnp.bfloat16), value_grad.astype(jnp.bfloat16)
        kv_grad[:, key_cols] = key_grad
        kv_grad[:, value_cols] = value_grad
        here = jnp.sum(
            key_grad.astype(jnp.float32) * key_full + value_grad.astype(jnp.float32) * value_full,
            axis=1,
            keepdims=True,
        )
        row_part = here if row_part is None else row_part + here
    row_ref[...] = jnp.transpose(jnp.broadcast_to(row_part, (tokens, 128)))[0:1, :]

    grad = kv_grad[...]
    tile = half // 4
    for t in range(4):
        rows = pl.ds(pl.multiple_of((1 - me) * half + t * tile, tile), tile)
        sib_ref[:, pl.ds(t * tile, tile)] = lax.dot_general(
            grad, weight[rows, :], LAST, preferred_element_type=jnp.float32
        ).astype(jnp.bfloat16)
    for t in range(4):
        rows = pl.ds(pl.multiple_of(me * half + t * tile, tile), tile)
        own_ref[:, pl.ds(t * tile, tile)] = lax.dot_general(
            grad, weight[rows, :], LAST, preferred_element_type=jnp.float32
        )


def chip_kernel(parts, own_ref, sib_ref, kept_ref, *big_refs):
    feats = kept_ref.shape[1]
    section = lax.axis_index("section")
    for k in range(parts):
        at = pl.multiple_of(partner(section, k, parts) * feats, feats)
        total = own_ref[:, pl.ds(at, feats)] + sib_ref[:, pl.ds(at, feats)].astype(jnp.float32)
        if k == 0:
            kept_ref[...] = total
        else:
            big_refs[k - 1][...] = total.astype(jnp.bfloat16)


def gain_kernel(parts, row_ref, row_sib_ref, inv_ref, *refs):
    chunk_refs, total_refs, small_refs = refs[:parts], refs[parts : 2 * parts], refs[2 * parts :]
    feats = chunk_refs[0].shape[1]
    inv_rms = inv_ref[...]
    row = row_ref[...] + row_sib_ref[...]
    for k in range(parts):
        normed = chunk_refs[k][...].astype(jnp.float32) * inv_rms
        total = total_refs[k][...].astype(jnp.float32)
        small_refs[k][:, pl.ds(0, feats)] = jnp.sum(total * normed, axis=0, keepdims=True)
        small_refs[k][:, pl.ds(feats, row.shape[1])] = row


def last_kernel(parts, width, kept_ref, *refs):
    big_refs = refs[: parts - 1]
    chunk_ref, inv_ref, gain_ref, row_ref, enc_ref = refs[parts - 1 :]
    tokens, feats = chunk_ref.shape
    grad = kept_ref[...]
    for ref in big_refs:
        grad = grad + ref[...].astype(jnp.float32)
    inv_rms = inv_ref[...]
    me = lax.axis_index("sec") * parts + lax.axis_index("section")
    at = pl.multiple_of(me * feats, feats)
    gain = gain_ref[:, pl.ds(at, feats)]
    normed = chunk_ref[...].astype(jnp.float32) * inv_rms
    row_dot = jnp.transpose(jnp.broadcast_to(row_ref[...], (128, tokens)))[:, 0:1]
    enc_ref[...] = (inv_rms * (gain * grad - normed * (row_dot / width))).astype(jnp.bfloat16)


def per_device(sizes, enc_states, norm_gain, kv_weight, queries, attn_cotangent, target_lengths):
    cores, parts, seqs = sizes
    rows = enc_states[0]
    tokens, feats = rows.shape
    weight = kv_weight[0]
    width = weight.shape[0]
    half = width // 2
    query, cot = queries[0, 0], attn_cotangent[0, 0]
    dec = query.shape[0]
    heads = query.shape[1] // HS
    gain = norm_gain.reshape(1, width)
    swap = [(0, 1), (1, 0)]

    def to_section(x, step):
        return lax.ppermute(x, "section", [(i, partner(i, step, parts)) for i in range(parts)])

    def to_core(x):
        return lax.ppermute(x, "sec", swap)

    square = pl.pallas_call(
        first_kernel,
        out_shape=jax.ShapeDtypeStruct((tokens, 1), jnp.float32),
        in_specs=[VMEM, ANY],
        out_specs=VMEM,
        compiler_params=pltpu.CompilerParams(vmem_limit_bytes=16 << 20),
        cost_estimate=pl.CostEstimate(
            flops=20_000_000_000, bytes_accessed=2 * rows.size, transcendentals=0
        ),
        name="first",
    )(rows, weight)
    flops = 2 * tokens * width * weight.shape[1]
    chunks = [rows]
    for k in range(1, parts):
        chunks.append(lax.optimization_barrier((to_section(rows, k), square))[0])
    others = [to_core(c) for c in chunks]
    att, sib, own, inv_rms, row = pl.pallas_call(
        functools.partial(main_kernel, parts, heads),
        out_shape=(
            jax.ShapeDtypeStruct(query.shape, jnp.bfloat16),
            jax.ShapeDtypeStruct((tokens, half), jnp.bfloat16),
            jax.ShapeDtypeStruct((tokens, half), jnp.float32),
            jax.ShapeDtypeStruct((tokens, 1), jnp.float32),
            jax.ShapeDtypeStruct((1, tokens), jnp.float32),
        ),
        in_specs=[SMEM] + [VMEM] * (1 + 2 * parts) + [VMEM, VMEM, VMEM, VMEM],
        out_specs=(VMEM,) * 5,
        scratch_shapes=[
            pltpu.VMEM((tokens, width), jnp.bfloat16),
            pltpu.VMEM((tokens, weight.shape[1]), jnp.float32),
            pltpu.VMEM((tokens, weight.shape[1]), jnp.bfloat16),
        ],
        compiler_params=pltpu.CompilerParams(vmem_limit_bytes=16 << 20),
        cost_estimate=pl.CostEstimate(
            flops=3 * flops, bytes_accessed=2 * weight.size, transcendentals=dec * tokens * heads
        ),
        name="main",
    )(target_lengths, square, *chunks, *others, gain, weight, query, cot)

    row_sib = to_core(row)
    sib_in = to_core(sib)

    kept, *big = pl.pallas_call(
        functools.partial(chip_kernel, parts),
        out_shape=(jax.ShapeDtypeStruct((tokens, feats), jnp.float32),)
        + (jax.ShapeDtypeStruct((tokens, feats), jnp.bfloat16),) * (parts - 1),
        in_specs=[VMEM] * 2,
        out_specs=(VMEM,) * parts,
        compiler_params=pltpu.CompilerParams(vmem_limit_bytes=16 << 20),
        cost_estimate=pl.CostEstimate(
            flops=2 * tokens * half, bytes_accessed=8 * tokens * half, transcendentals=0
        ),
        name="chip",
    )(own, sib_in)
    small = pl.pallas_call(
        functools.partial(gain_kernel, parts),
        out_shape=(jax.ShapeDtypeStruct((1, feats + tokens), jnp.float32),) * parts,
        in_specs=[VMEM] * (3 + 2 * parts),
        out_specs=(VMEM,) * parts,
        compiler_params=pltpu.CompilerParams(vmem_limit_bytes=16 << 20),
        cost_estimate=pl.CostEstimate(
            flops=20_000_000_000, bytes_accessed=8 * tokens * half, transcendentals=0
        ),
        name="gain",
    )(row, row_sib, inv_rms, *chunks, kept, *big)

    big_in = [to_section(big[k - 1], k) for k in range(1, parts)]
    gain_row = direct_sum(small, "section", parts)
    gain_term, row_dot = gain_row[0, :feats], gain_row[:, feats:]
    enc_grad = pl.pallas_call(
        functools.partial(last_kernel, parts, width),
        out_shape=jax.ShapeDtypeStruct((tokens, feats), jnp.bfloat16),
        in_specs=[VMEM] * (4 + parts),
        out_specs=VMEM,
        compiler_params=pltpu.CompilerParams(vmem_limit_bytes=8 << 20),
        cost_estimate=pl.CostEstimate(
            flops=10 * tokens * feats, bytes_accessed=16 * tokens * feats, transcendentals=0
        ),
        name="last",
    )(kept, *big_in, rows, inv_rms, gain, row_dot)
    if seqs <= 8:
        piece = feats // seqs
        dp = lax.axis_index("dp")
        owned = [
            lax.dynamic_slice_in_dim(gain_term, partner(dp, k, seqs) * piece, piece, 0)
            for k in range(seqs)
        ]
        came = [
            lax.ppermute(owned[k], "dp", [(i, partner(i, k, seqs)) for i in range(seqs)])
            for k in reversed(range(1, seqs))
        ]
        enc_grad, first = lax.optimization_barrier((enc_grad, owned[0]))
        gain_grad = tree_sum([first] + came)
    else:
        gain_grad = lax.psum_scatter(gain_term, "dp", scatter_dimension=0, tiled=True)
    return (att[None, None], enc_grad[None], gain_grad, row_dot)


def solution(mesh):
    sizes = tuple(mesh.shape[a] for a in ("sec", "section", "dp"))
    placed = (
        P("dp", None, ("sec", "section")),
        P(),
        P("sec", None, "section"),
        P("sec", "dp", None, "section"),
        P("sec", "dp", None, "section"),
        P("dp"),
    )
    return jax.shard_map(
        functools.partial(per_device, sizes),
        mesh=mesh,
        in_specs=placed,
        out_specs=(
            P("sec", "dp", None, "section"),
            P("dp", None, ("sec", "section")),
            P(("sec", "section", "dp")),
            P("dp", None),
        ),
        check_vma=False,
    )
```

```python
import functools

import jax
import jax.numpy as jnp
from jax import lax
from jax.experimental import pallas as pl
from jax.experimental.pallas import tpu as pltpu
from jax.sharding import PartitionSpec as P

HS = 256
EPS = 1e-06
LAST = (((1,), (1,)), ((), ()))
FIRST = (((0,), (0,)), ((), ()))
VMEM = pl.BlockSpec(memory_space=pltpu.VMEM)
SMEM = pl.BlockSpec(memory_space=pltpu.SMEM)
ANY = pl.BlockSpec(memory_space=pl.ANY)


def partner(index, step, count):
    return index ^ step


def tree_sum(terms):
    while len(terms) > 1:
        terms = [terms[i] + terms[i + 1] for i in range(0, len(terms), 2)]
    return terms[0]


def direct_sum(terms, axis, count):
    perms = [[(i, partner(i, k, count)) for i in range(count)] for k in range(count)]
    return tree_sum([terms[0]] + [lax.ppermute(terms[k], axis, perms[k]) for k in range(1, count)])


def first_kernel(token_ref):
    token_ref[...] = jnp.zeros_like(token_ref)


def main_kernel(
    parts,
    heads,
    length_ref,
    token_ref,
    *refs,
):
    chunk_refs = refs[: 2 * parts]
    (gain_ref, weight, query_ref, cot_ref) = refs[2 * parts : 2 * parts + 4]
    (att_ref, sib_ref, own_ref, inv_ref, row_ref) = refs[2 * parts + 4 : 2 * parts + 9]
    (memory, kv, kv_grad) = refs[2 * parts + 9 :]
    tokens, feats = chunk_refs[0].shape
    width = weight.shape[0]
    half = width // 2

    square = None
    for ref in chunk_refs:
        x = ref[...].astype(jnp.float32)
        part = jnp.sum((x * x).reshape(tokens, feats // 128, 128), axis=1)
        square = part if square is None else square + part
    square = jnp.sum(square, axis=1, keepdims=True)
    inv_rms = lax.rsqrt(square / width + EPS)
    inv_ref[...] = inv_rms
    me, section = lax.axis_index("sec"), lax.axis_index("section")
    for j, ref in enumerate(chunk_refs):
        owner = me if j < parts else 1 - me
        at = pl.multiple_of((owner * parts + partner(section, j % parts, parts)) * feats, feats)
        normed = ref[...].astype(jnp.float32) * inv_rms
        memory[:, pl.ds(at, feats)] = (normed * gain_ref[:, pl.ds(at, feats)]).astype(jnp.bfloat16)

    kv[...] = jnp.dot(memory[...], weight[...], preferred_element_type=jnp.float32)

    scale = HS ** (-0.5)
    live = lax.broadcasted_iota(jnp.int32, (query_ref.shape[0], HS), 0) < length_ref[0]
    row_part = None
    for h in range(heads):
        cols = pl.ds(h * HS, HS)
        key_cols, value_cols = pl.ds(2 * h * HS, HS), pl.ds((2 * h + 1) * HS, HS)
        key_full, value_full = kv[:, key_cols], kv[:, value_cols]
        key_rows, value_rows = key_full.astype(jnp.bfloat16), value_full.astype(jnp.bfloat16)
        query = query_ref[:, cols]
        cot = cot_ref[:, cols]
        masked = jnp.where(live, cot, jnp.zeros_like(cot))
        scores = lax.dot_general(key_rows, query, LAST, preferred_element_type=jnp.float32) * scale
        exponent = jnp.exp(scores)
        attention = exponent * (1.0 / jnp.sum(exponent, axis=0, keepdims=True))
        weights_b = attention.astype(jnp.bfloat16)
        att_ref[:, cols] = lax.dot_general(
            weights_b, value_rows, FIRST, preferred_element_type=jnp.float32
        ).astype(jnp.bfloat16)
        back = lax.dot_general(value_rows, masked, LAST, preferred_element_type=jnp.float32)
        mean = jnp.sum(attention * back, axis=0, keepdims=True)
        score_grad = (attention * (back - mean) * scale).astype(jnp.bfloat16)
        key_grad = jnp.dot(score_grad, query, preferred_element_type=jnp.float32)
        value_grad = jnp.dot(weights_b, masked, preferred_element_type=jnp.float32)
        key_grad, value_grad = key_grad.astype(jnp.bfloat16), value_grad.astype(jnp.bfloat16)
        kv_grad[:, key_cols] = key_grad
        kv_grad[:, value_cols] = value_grad
        here = jnp.sum(
            key_grad.astype(jnp.float32) * key_full + value_grad.astype(jnp.float32) * value_full,
            axis=1,
            keepdims=True,
        )
        row_part = here if row_part is None else row_part + here
    row_ref[...] = jnp.transpose(jnp.broadcast_to(row_part, (tokens, 128)))[0:1, :]

    grad = kv_grad[...]
    tile = half // 4
    for t in range(4):
        rows = pl.ds(pl.multiple_of((1 - me) * half + t * tile, tile), tile)
        sib_ref[:, pl.ds(t * tile, tile)] = lax.dot_general(
            grad, weight[rows, :], LAST, preferred_element_type=jnp.float32
        ).astype(jnp.bfloat16)
    for t in range(4):
        rows = pl.ds(pl.multiple_of(me * half + t * tile, tile), tile)
        own_ref[:, pl.ds(t * tile, tile)] = lax.dot_general(
            grad, weight[rows, :], LAST, preferred_element_type=jnp.float32
        )


def chip_kernel(parts, own_ref, sib_ref, kept_ref, *big_refs):
    feats = kept_ref.shape[1]
    section = lax.axis_index("section")
    for k in range(parts):
        at = pl.multiple_of(partner(section, k, parts) * feats, feats)
        total = own_ref[:, pl.ds(at, feats)] + sib_ref[:, pl.ds(at, feats)].astype(jnp.float32)
        if k == 0:
            kept_ref[...] = total
        else:
            big_refs[k - 1][...] = total.astype(jnp.bfloat16)


def gain_kernel(parts, row_ref, row_sib_ref, inv_ref, *refs):
    chunk_refs, total_refs, small_refs = refs[:parts], refs[parts : 2 * parts], refs[2 * parts :]
    feats = chunk_refs[0].shape[1]
    inv_rms = inv_ref[...]
    row = row_ref[...] + row_sib_ref[...]
    for k in range(parts):
        normed = chunk_refs[k][...].astype(jnp.float32) * inv_rms
        total = total_refs[k][...].astype(jnp.float32)
        small_refs[k][:, pl.ds(0, feats)] = jnp.sum(total * normed, axis=0, keepdims=True)
        small_refs[k][:, pl.ds(feats, row.shape[1])] = row


def last_kernel(parts, width, kept_ref, *refs):
    big_refs = refs[: parts - 1]
    chunk_ref, inv_ref, gain_ref, row_ref, enc_ref = refs[parts - 1 :]
    tokens, feats = chunk_ref.shape
    grad = kept_ref[...]
    for ref in big_refs:
        grad = grad + ref[...].astype(jnp.float32)
    inv_rms = inv_ref[...]
    me = lax.axis_index("sec") * parts + lax.axis_index("section")
    at = pl.multiple_of(me * feats, feats)
    gain = gain_ref[:, pl.ds(at, feats)]
    normed = chunk_ref[...].astype(jnp.float32) * inv_rms
    row_dot = jnp.transpose(jnp.broadcast_to(row_ref[...], (128, tokens)))[:, 0:1]
    enc_ref[...] = (inv_rms * (gain * grad - normed * (row_dot / width))).astype(jnp.bfloat16)


def per_device(sizes, enc_states, norm_gain, kv_weight, queries, attn_cotangent, target_lengths):
    cores, parts, seqs = sizes
    rows = enc_states[0]
    tokens, feats = rows.shape
    weight = kv_weight[0]
    width = weight.shape[0]
    half = width // 2
    query, cot = queries[0, 0], attn_cotangent[0, 0]
    dec = query.shape[0]
    heads = query.shape[1] // HS
    gain = norm_gain.reshape(1, width)
    swap = [(0, 1), (1, 0)]

    def to_section(x, step):
        return lax.ppermute(x, "section", [(i, partner(i, step, parts)) for i in range(parts)])

    def to_core(x):
        return lax.ppermute(x, "sec", swap)

    token = pl.pallas_call(
        first_kernel,
        out_shape=jax.ShapeDtypeStruct((8, 128), jnp.float32),
        out_specs=VMEM,
        compiler_params=pltpu.CompilerParams(vmem_limit_bytes=1 << 20),
        cost_estimate=pl.CostEstimate(flops=20_000_000_000, bytes_accessed=4096, transcendentals=0),
        name="first",
    )()
    flops = 2 * tokens * width * weight.shape[1]
    chunks = [rows]
    for k in range(1, parts):
        chunks.append(lax.optimization_barrier((to_section(rows, k), token))[0])
    others = [to_core(c) for c in chunks]
    att, sib, own, inv_rms, row = pl.pallas_call(
        functools.partial(main_kernel, parts, heads),
        out_shape=(
            jax.ShapeDtypeStruct(query.shape, jnp.bfloat16),
            jax.ShapeDtypeStruct((tokens, half), jnp.bfloat16),
            jax.ShapeDtypeStruct((tokens, half), jnp.float32),
            jax.ShapeDtypeStruct((tokens, 1), jnp.float32),
            jax.ShapeDtypeStruct((1, tokens), jnp.float32),
        ),
        in_specs=[SMEM, ANY] + [VMEM] * (2 * parts) + [VMEM, VMEM, VMEM, VMEM],
        out_specs=(VMEM,) * 5,
        scratch_shapes=[
            pltpu.VMEM((tokens, width), jnp.bfloat16),
            pltpu.VMEM((tokens, weight.shape[1]), jnp.float32),
            pltpu.VMEM((tokens, weight.shape[1]), jnp.bfloat16),
        ],
        compiler_params=pltpu.CompilerParams(vmem_limit_bytes=16 << 20),
        cost_estimate=pl.CostEstimate(
            flops=3 * flops, bytes_accessed=2 * weight.size, transcendentals=dec * tokens * heads
        ),
        name="main",
    )(target_lengths, token, *chunks, *others, gain, weight, query, cot)

    row_sib = to_core(row)
    sib_in = to_core(sib)

    kept, *big = pl.pallas_call(
        functools.partial(chip_kernel, parts),
        out_shape=(jax.ShapeDtypeStruct((tokens, feats), jnp.float32),)
        + (jax.ShapeDtypeStruct((tokens, feats), jnp.bfloat16),) * (parts - 1),
        in_specs=[VMEM] * 2,
        out_specs=(VMEM,) * parts,
        compiler_params=pltpu.CompilerParams(vmem_limit_bytes=16 << 20),
        cost_estimate=pl.CostEstimate(
            flops=2 * tokens * half, bytes_accessed=8 * tokens * half, transcendentals=0
        ),
        name="chip",
    )(own, sib_in)
    small = pl.pallas_call(
        functools.partial(gain_kernel, parts),
        out_shape=(jax.ShapeDtypeStruct((1, feats + tokens), jnp.float32),) * parts,
        in_specs=[VMEM] * (3 + 2 * parts),
        out_specs=(VMEM,) * parts,
        compiler_params=pltpu.CompilerParams(vmem_limit_bytes=16 << 20),
        cost_estimate=pl.CostEstimate(
            flops=20_000_000_000, bytes_accessed=8 * tokens * half, transcendentals=0
        ),
        name="gain",
    )(row, row_sib, inv_rms, *chunks, kept, *big)

    big_in = [to_section(big[k - 1], k) for k in range(1, parts)]
    gain_row = direct_sum(small, "section", parts)
    gain_term, row_dot = gain_row[0, :feats], gain_row[:, feats:]
    enc_grad = pl.pallas_call(
        functools.partial(last_kernel, parts, width),
        out_shape=jax.ShapeDtypeStruct((tokens, feats), jnp.bfloat16),
        in_specs=[VMEM] * (4 + parts),
        out_specs=VMEM,
        compiler_params=pltpu.CompilerParams(vmem_limit_bytes=8 << 20),
        cost_estimate=pl.CostEstimate(
            flops=10 * tokens * feats, bytes_accessed=16 * tokens * feats, transcendentals=0
        ),
        name="last",
    )(kept, *big_in, rows, inv_rms, gain, row_dot)
    if seqs <= 8:
        piece = feats // seqs
        dp = lax.axis_index("dp")
        owned = [
            lax.dynamic_slice_in_dim(gain_term, partner(dp, k, seqs) * piece, piece, 0)
            for k in range(seqs)
        ]
        came = [
            lax.ppermute(owned[k], "dp", [(i, partner(i, k, seqs)) for i in range(seqs)])
            for k in reversed(range(1, seqs))
        ]
        enc_grad, first = lax.optimization_barrier((enc_grad, owned[0]))
        gain_grad = tree_sum([first] + came)
    else:
        gain_grad = lax.psum_scatter(gain_term, "dp", scatter_dimension=0, tiled=True)
    return (att[None, None], enc_grad[None], gain_grad, row_dot)


def solution(mesh):
    sizes = tuple(mesh.shape[a] for a in ("sec", "section", "dp"))
    placed = (
        P("dp", None, ("sec", "section")),
        P(),
        P("sec", None, "section"),
        P("sec", "dp", None, "section"),
        P("sec", "dp", None, "section"),
        P("dp"),
    )
    return jax.shard_map(
        functools.partial(per_device, sizes),
        mesh=mesh,
        in_specs=placed,
        out_specs=(
            P("sec", "dp", None, "section"),
            P("dp", None, ("sec", "section")),
            P(("sec", "section", "dp")),
            P("dp", None),
        ),
        check_vma=False,
    )
```

```python
import functools

import jax
import jax.numpy as jnp
from jax import lax
from jax.experimental import pallas as pl
from jax.experimental.pallas import tpu as pltpu
from jax.sharding import PartitionSpec as P

HS = 256
EPS = 1e-06
LAST = (((1,), (1,)), ((), ()))
FIRST = (((0,), (0,)), ((), ()))
VMEM = pl.BlockSpec(memory_space=pltpu.VMEM)
SMEM = pl.BlockSpec(memory_space=pltpu.SMEM)
ANY = pl.BlockSpec(memory_space=pl.ANY)


def reverse_bits(step, count):
    out, bit = 0, 1
    while bit < count:
        out = 2 * out + (1 if step & bit else 0)
        bit *= 2
    return out


def section_step(core, step, count):
    if isinstance(core, int):
        return reverse_bits(step, count) if core else step
    return jnp.where(core == 0, step, reverse_bits(step, count))


def tree_sum(terms):
    while len(terms) > 1:
        terms = [terms[i] + terms[i + 1] for i in range(0, len(terms), 2)]
    return terms[0]


def first_kernel(token_ref):
    token_ref[...] = jnp.zeros_like(token_ref)


def main_kernel(
    parts,
    heads,
    length_ref,
    token_ref,
    *refs,
):
    chunk_refs = refs[: 2 * parts]
    (gain_ref, weight, query_ref, cot_ref) = refs[2 * parts : 2 * parts + 4]
    (att_ref, sib_ref, kv_grad, inv_ref, row_ref) = refs[2 * parts + 4 : 2 * parts + 9]
    (memory, kv) = refs[2 * parts + 9 :]
    tokens, feats = chunk_refs[0].shape
    width = weight.shape[0]
    half = width // 2

    square = None
    for ref in chunk_refs:
        x = ref[...].astype(jnp.float32)
        x = x * x
        for i in range(0, feats, 128):
            square = x[:, i : i + 128] if square is None else square + x[:, i : i + 128]
    square = jnp.sum(square, axis=1, keepdims=True)
    inv_rms = lax.rsqrt(square / width + EPS)
    inv_ref[...] = inv_rms
    me, section = lax.axis_index("sec"), lax.axis_index("section")
    for j, ref in enumerate(chunk_refs):
        owner = me if j < parts else 1 - me
        peer = section ^ section_step(owner, j % parts, parts)
        at = pl.multiple_of((owner * parts + peer) * feats, feats)
        normed = ref[...].astype(jnp.float32) * inv_rms
        memory[:, pl.ds(at, feats)] = (normed * gain_ref[:, pl.ds(at, feats)]).astype(jnp.bfloat16)

    kv[...] = jnp.dot(memory[...], weight[...], preferred_element_type=jnp.float32)

    scale = HS ** (-0.5)
    live = lax.broadcasted_iota(jnp.int32, (query_ref.shape[0], HS), 0) < length_ref[0]
    row_part = None
    for h in range(heads):
        cols = pl.ds(h * HS, HS)
        key_cols, value_cols = pl.ds(2 * h * HS, HS), pl.ds((2 * h + 1) * HS, HS)
        key_full, value_full = kv[:, key_cols], kv[:, value_cols]
        key_rows, value_rows = key_full.astype(jnp.bfloat16), value_full.astype(jnp.bfloat16)
        query = query_ref[:, cols]
        cot = cot_ref[:, cols]
        masked = jnp.where(live, cot, jnp.zeros_like(cot))
        scores = lax.dot_general(key_rows, query, LAST, preferred_element_type=jnp.float32) * scale
        exponent = jnp.exp(scores)
        attention = exponent * (1.0 / jnp.sum(exponent, axis=0, keepdims=True))
        weights_b = attention.astype(jnp.bfloat16)
        att_ref[:, cols] = lax.dot_general(
            weights_b, value_rows, FIRST, preferred_element_type=jnp.float32
        ).astype(jnp.bfloat16)
        back = lax.dot_general(value_rows, masked, LAST, preferred_element_type=jnp.float32)
        mean = jnp.sum(attention * back, axis=0, keepdims=True)
        score_grad = (attention * (back - mean) * scale).astype(jnp.bfloat16)
        key_grad = jnp.dot(score_grad, query, preferred_element_type=jnp.float32)
        value_grad = jnp.dot(weights_b, masked, preferred_element_type=jnp.float32)
        key_grad, value_grad = key_grad.astype(jnp.bfloat16), value_grad.astype(jnp.bfloat16)
        kv_grad[:, key_cols] = key_grad
        kv_grad[:, value_cols] = value_grad
        here = jnp.sum(
            key_grad.astype(jnp.float32) * key_full + value_grad.astype(jnp.float32) * value_full,
            axis=1,
            keepdims=True,
        )
        row_part = here if row_part is None else row_part + here
    row_ref[...] = jnp.transpose(jnp.broadcast_to(row_part, (tokens, 128)))[0:1, :]

    grad = kv_grad[...]
    tile = half // 4
    for t in range(4):
        rows = pl.ds(pl.multiple_of((1 - me) * half + t * tile, tile), tile)
        sib_ref[:, pl.ds(t * tile, tile)] = lax.dot_general(
            grad, weight[rows, :], LAST, preferred_element_type=jnp.float32
        ).astype(jnp.bfloat16)


def back_kernel(grad_ref, weight, own_ref):
    half = own_ref.shape[1]
    me = lax.axis_index("sec")
    grad = grad_ref[...]
    tile = half // 4
    for t in range(4):
        rows = pl.ds(pl.multiple_of(me * half + t * tile, tile), tile)
        own_ref[:, pl.ds(t * tile, tile)] = lax.dot_general(
            grad, weight[rows, :], LAST, preferred_element_type=jnp.float32
        )


def chip_kernel(parts, own_ref, sib_ref, kept_ref, *big_refs):
    feats = kept_ref.shape[1]
    me, section = lax.axis_index("sec"), lax.axis_index("section")
    for k in range(parts):
        at = pl.multiple_of((section ^ section_step(me, k, parts)) * feats, feats)
        total = own_ref[:, pl.ds(at, feats)] + sib_ref[:, pl.ds(at, feats)].astype(jnp.float32)
        if k == 0:
            kept_ref[...] = total
        else:
            big_refs[k - 1][...] = total.astype(jnp.bfloat16)


def gain_kernel(parts, row_ref, row_sib_ref, inv_ref, *refs):
    chunk_refs, total_refs, small_refs = refs[:parts], refs[parts : 2 * parts], refs[2 * parts :]
    feats = chunk_refs[0].shape[1]
    inv_rms = inv_ref[...]
    row = row_ref[...] + row_sib_ref[...]
    for k in range(parts):
        normed = chunk_refs[k][...].astype(jnp.float32) * inv_rms
        total = total_refs[k][...].astype(jnp.float32)
        small_refs[k][:, pl.ds(0, feats)] = jnp.sum(total * normed, axis=0, keepdims=True)
        small_refs[k][:, pl.ds(feats, row.shape[1])] = row


def total_kernel(kept_ref, *refs):
    total = kept_ref[...]
    for ref in refs[:-1]:
        total = total + ref[...].astype(jnp.float32)
    refs[-1][...] = total


def last_kernel(parts, width, grad_ref, chunk_ref, inv_ref, gain_ref, *refs):
    small_refs, gain_refs, (enc_ref, row_ref, *gain_out) = refs[:parts], refs[parts:-3], refs[-3:]
    if not gain_refs:
        small_refs, (enc_ref, row_ref), gain_out = refs[:parts], refs[-2:], ()
    tokens, feats = chunk_ref.shape
    core = lax.axis_index("sec")
    rows = [ref[:, pl.ds(feats, tokens)] for ref in small_refs]
    row = tree_sum(
        [jnp.where(core == 0, rows[k], rows[reverse_bits(k, parts)]) for k in range(parts)]
    )
    row_ref[...] = row
    grad = grad_ref[...]
    inv_rms = inv_ref[...]
    at = pl.multiple_of((core * parts + lax.axis_index("section")) * feats, feats)
    gain = gain_ref[:, pl.ds(at, feats)]
    normed = chunk_ref[...].astype(jnp.float32) * inv_rms
    row_dot = jnp.transpose(jnp.broadcast_to(row, (128, tokens)))[:, 0:1]
    enc_ref[...] = (inv_rms * (gain * grad - normed * (row_dot / width))).astype(jnp.bfloat16)
    for ref in gain_out:
        ref[...] = tree_sum([g[...] for g in gain_refs])


def per_device(sizes, enc_states, norm_gain, kv_weight, queries, attn_cotangent, target_lengths):
    cores, parts, seqs = sizes
    rows = enc_states[0]
    tokens, feats = rows.shape
    weight = kv_weight[0]
    width = weight.shape[0]
    half = width // 2
    query, cot = queries[0, 0], attn_cotangent[0, 0]
    dec = query.shape[0]
    heads = query.shape[1] // HS
    gain = norm_gain.reshape(1, width)
    swap = [(0, 1), (1, 0)]

    def to_section(x, step):
        pairs = [
            (c * parts + i, c * parts + (i ^ section_step(c, step, parts)))
            for c in range(cores)
            for i in range(parts)
        ]
        return lax.ppermute(x, ("sec", "section"), pairs)

    def to_core(x):
        return lax.ppermute(x, "sec", swap)

    token = pl.pallas_call(
        first_kernel,
        out_shape=jax.ShapeDtypeStruct((8, 128), jnp.float32),
        out_specs=VMEM,
        compiler_params=pltpu.CompilerParams(vmem_limit_bytes=1 << 20),
        cost_estimate=pl.CostEstimate(flops=20_000_000_000, bytes_accessed=4096, transcendentals=0),
        name="first",
    )()
    flops = 2 * tokens * width * weight.shape[1]
    chunks = [rows]
    for k in range(1, parts):
        chunks.append(lax.optimization_barrier((to_section(rows, k), token))[0])
    others = [to_core(c) for c in chunks]
    att, sib, kv_grad, inv_rms, row = pl.pallas_call(
        functools.partial(main_kernel, parts, heads),
        out_shape=(
            jax.ShapeDtypeStruct(query.shape, jnp.bfloat16),
            jax.ShapeDtypeStruct((tokens, half), jnp.bfloat16),
            jax.ShapeDtypeStruct((tokens, weight.shape[1]), jnp.bfloat16),
            jax.ShapeDtypeStruct((tokens, 1), jnp.float32),
            jax.ShapeDtypeStruct((1, tokens), jnp.float32),
        ),
        in_specs=[SMEM, ANY] + [VMEM] * (2 * parts) + [VMEM, VMEM, VMEM, VMEM],
        out_specs=(VMEM,) * 5,
        scratch_shapes=[
            pltpu.VMEM((tokens, width), jnp.bfloat16),
            pltpu.VMEM((tokens, weight.shape[1]), jnp.float32),
        ],
        compiler_params=pltpu.CompilerParams(vmem_limit_bytes=16 << 20),
        cost_estimate=pl.CostEstimate(
            flops=3 * flops, bytes_accessed=2 * weight.size, transcendentals=dec * tokens * heads
        ),
        name="main",
    )(target_lengths, token, *chunks, *others, gain, weight, query, cot)

    own = pl.pallas_call(
        back_kernel,
        out_shape=jax.ShapeDtypeStruct((tokens, half), jnp.float32),
        in_specs=[VMEM, VMEM],
        out_specs=VMEM,
        compiler_params=pltpu.CompilerParams(vmem_limit_bytes=16 << 20),
        cost_estimate=pl.CostEstimate(
            flops=flops // 2, bytes_accessed=weight.size, transcendentals=0
        ),
        name="back",
    )(kv_grad, weight)
    row_sib = to_core(row)
    sib_in = to_core(sib)

    kept, *big = pl.pallas_call(
        functools.partial(chip_kernel, parts),
        out_shape=(jax.ShapeDtypeStruct((tokens, feats), jnp.float32),)
        + (jax.ShapeDtypeStruct((tokens, feats), jnp.bfloat16),) * (parts - 1),
        in_specs=[VMEM] * 2,
        out_specs=(VMEM,) * parts,
        compiler_params=pltpu.CompilerParams(vmem_limit_bytes=16 << 20),
        cost_estimate=pl.CostEstimate(
            flops=2 * tokens * half, bytes_accessed=8 * tokens * half, transcendentals=0
        ),
        name="chip",
    )(own, sib_in)
    small = pl.pallas_call(
        functools.partial(gain_kernel, parts),
        out_shape=(jax.ShapeDtypeStruct((1, feats + tokens), jnp.float32),) * parts,
        in_specs=[VMEM] * (3 + 2 * parts),
        out_specs=(VMEM,) * parts,
        compiler_params=pltpu.CompilerParams(vmem_limit_bytes=16 << 20),
        cost_estimate=pl.CostEstimate(
            flops=20_000_000_000, bytes_accessed=8 * tokens * half, transcendentals=0
        ),
        name="gain",
    )(row, row_sib, inv_rms, *chunks, kept, *big)

    big_in = [to_section(big[k - 1], k) for k in range(1, parts)]
    small_in = [small[0]] + [to_section(small[k], k) for k in range(1, parts)]
    gain_term = tree_sum([x[:, :feats] for x in small_in])
    direct = seqs <= 8 and (feats // seqs) % 128 == 0
    pieces = []
    if direct:
        piece = feats // seqs
        dp = lax.axis_index("dp")
        pieces = [lax.dynamic_slice_in_dim(gain_term, dp * piece, piece, 1)]
        for k in reversed(range(1, seqs)):
            send = lax.dynamic_slice_in_dim(gain_term, (dp ^ k) * piece, piece, 1)
            pieces.append(lax.ppermute(send, "dp", [(i, i ^ k) for i in range(seqs)]))
    total = pl.pallas_call(
        total_kernel,
        out_shape=jax.ShapeDtypeStruct((tokens, feats), jnp.float32),
        in_specs=[VMEM] * parts,
        out_specs=VMEM,
        compiler_params=pltpu.CompilerParams(vmem_limit_bytes=8 << 20),
        cost_estimate=pl.CostEstimate(flops=20_000_000_000, bytes_accessed=4096, transcendentals=0),
        name="total",
    )(kept, *big_in)
    enc_grad, row_dot, *gain_grad = pl.pallas_call(
        functools.partial(last_kernel, parts, width),
        out_shape=(
            jax.ShapeDtypeStruct((tokens, feats), jnp.bfloat16),
            jax.ShapeDtypeStruct((1, tokens), jnp.float32),
        )
        + ((jax.ShapeDtypeStruct(pieces[0].shape, jnp.float32),) if direct else ()),
        in_specs=[VMEM] * (4 + parts + len(pieces)),
        out_specs=(VMEM,) * (3 if direct else 2),
        compiler_params=pltpu.CompilerParams(vmem_limit_bytes=8 << 20),
        cost_estimate=pl.CostEstimate(
            flops=10 * tokens * feats, bytes_accessed=16 * tokens * feats, transcendentals=0
        ),
        name="last",
    )(total, rows, inv_rms, gain, *small_in, *pieces)
    if direct:
        gain_grad = gain_grad[0][0]
    else:
        gain_grad = lax.psum_scatter(gain_term[0], "dp", scatter_dimension=0, tiled=True)
    return (att[None, None], enc_grad[None], gain_grad, row_dot)


def solution(mesh):
    sizes = tuple(mesh.shape[a] for a in ("sec", "section", "dp"))
    placed = (
        P("dp", None, ("sec", "section")),
        P(),
        P("sec", None, "section"),
        P("sec", "dp", None, "section"),
        P("sec", "dp", None, "section"),
        P("dp"),
    )
    return jax.shard_map(
        functools.partial(per_device, sizes),
        mesh=mesh,
        in_specs=placed,
        out_specs=(
            P("sec", "dp", None, "section"),
            P("dp", None, ("sec", "section")),
            P(("sec", "section", "dp")),
            P("dp", None),
        ),
        check_vma=False,
    )
```

```python
import functools

import jax
import jax.numpy as jnp
from jax import lax
from jax.experimental import pallas as pl
from jax.experimental.pallas import tpu as pltpu
from jax.sharding import PartitionSpec as P

HS = 256
EPS = 1e-06
ROW_TERMS = 3
LAST = (((1,), (1,)), ((), ()))
FIRST = (((0,), (0,)), ((), ()))
VMEM = pl.BlockSpec(memory_space=pltpu.VMEM)
SMEM = pl.BlockSpec(memory_space=pltpu.SMEM)
ANY = pl.BlockSpec(memory_space=pl.ANY)


def reverse_bits(step, count):
    out, bit = 0, 1
    while bit < count:
        out = 2 * out + (1 if step & bit else 0)
        bit *= 2
    return out


def section_step(core, step, count):
    if isinstance(core, int):
        return reverse_bits(step, count) if core else step
    return jnp.where(core == 0, step, reverse_bits(step, count))


def tree_sum(terms):
    while len(terms) > 1:
        terms = [terms[i] + terms[i + 1] for i in range(0, len(terms), 2)]
    return terms[0]


def first_kernel(token_ref):
    token_ref[...] = jnp.zeros_like(token_ref)


def project(parts, steps, chunk_refs, other_refs, gain_ref, weight, square, product_ref, started):
    me, section = lax.axis_index("sec"), lax.axis_index("section")
    feats = chunk_refs[0].shape[1]
    for refs, owner in ((chunk_refs, me), (other_refs, 1 - me)):
        for step, ref in zip(steps, refs, strict=True):
            peer = section ^ section_step(owner, step, parts)
            at = pl.multiple_of((owner * parts + peer) * feats, feats)
            cols = pl.ds(at, feats)
            x = ref[...].astype(jnp.float32)
            scaled = (x * gain_ref[:, cols]).astype(jnp.bfloat16)
            part = jnp.dot(scaled, weight[cols, :], preferred_element_type=jnp.float32)
            if started:
                product_ref[...] += part
            else:
                product_ref[...] = part
                started = True
            x = x * x
            for i in range(0, feats, 128):
                square = x[:, i : i + 128] if square is None else square + x[:, i : i + 128]
    return square


def early_kernel(parts, steps, *refs):
    count = len(steps)
    gain_ref, weight, product_ref, square_ref = refs[2 * count :]
    square_ref[...] = project(
        parts, steps, refs[:count], refs[count : 2 * count], gain_ref, weight, None, product_ref, False
    )


def main_kernel(
    parts,
    steps,
    heads,
    length_ref,
    token_ref,
    *refs,
):
    count = len(steps)
    chunk_refs, other_refs, refs = refs[:count], refs[count : 2 * count], refs[2 * count :]
    (product_ref, square_ref, gain_ref, weight, query_ref, cot_ref) = refs[:6]
    (att_hbm, sib_ref, kv_grad, inv_ref) = refs[6:10]
    (kv, att_ref, sem) = refs[10:]
    tokens = kv.shape[0]
    width = weight.shape[0]
    half = width // 2
    me = lax.axis_index("sec")

    kv[...] = product_ref[...]
    square = project(
        parts, steps, chunk_refs, other_refs, gain_ref, weight, square_ref[...], kv, True
    )
    inv_rms = lax.rsqrt(jnp.sum(square, axis=1, keepdims=True) / width + EPS)
    inv_ref[...] = inv_rms

    scale = HS ** (-0.5)
    live = lax.broadcasted_iota(jnp.int32, (query_ref.shape[0], HS), 0) < length_ref[0]
    row_part = None
    for h in range(heads):
        cols = pl.ds(h * HS, HS)
        key_cols, value_cols = pl.ds(2 * h * HS, HS), pl.ds((2 * h + 1) * HS, HS)
        key_full, value_full = kv[:, key_cols] * inv_rms, kv[:, value_cols] * inv_rms
        key_rows, value_rows = key_full.astype(jnp.bfloat16), value_full.astype(jnp.bfloat16)
        query = query_ref[:, cols]
        cot = cot_ref[:, cols]
        masked = jnp.where(live, cot, jnp.zeros_like(cot))
        scores = lax.dot_general(key_rows, query, LAST, preferred_element_type=jnp.float32) * scale
        exponent = jnp.exp(scores)
        attention = exponent * (1.0 / jnp.sum(exponent, axis=0, keepdims=True))
        weights_b = attention.astype(jnp.bfloat16)
        att_ref[:, cols] = lax.dot_general(
            weights_b, value_rows, FIRST, preferred_element_type=jnp.float32
        ).astype(jnp.bfloat16)
        back = lax.dot_general(value_rows, masked, LAST, preferred_element_type=jnp.float32)
        mean = jnp.sum(attention * back, axis=0, keepdims=True)
        score_grad = (attention * (back - mean) * scale).astype(jnp.bfloat16)
        key_grad = jnp.dot(score_grad, query, preferred_element_type=jnp.float32)
        value_grad = jnp.dot(weights_b, masked, preferred_element_type=jnp.float32)
        key_grad, value_grad = key_grad.astype(jnp.bfloat16), value_grad.astype(jnp.bfloat16)
        kv_grad[:, key_cols] = key_grad
        kv_grad[:, value_cols] = value_grad
        here = jnp.sum(
            key_grad.astype(jnp.float32) * key_full + value_grad.astype(jnp.float32) * value_full,
            axis=1,
            keepdims=True,
        )
        row_part = here if row_part is None else row_part + here
    att_out = pltpu.make_async_copy(att_ref, att_hbm, sem)
    att_out.start()
    rest = jnp.transpose(jnp.broadcast_to(row_part, (tokens, 128)))[0:8, :]
    pieces = jnp.zeros_like(rest)
    place = lax.broadcasted_iota(jnp.int32, rest.shape, 0)
    for i in range(ROW_TERMS):
        term = rest.astype(jnp.bfloat16).astype(jnp.float32)
        pieces = jnp.where(place == i, term, pieces)
        rest = rest - term
    sib_ref[pl.ds(tokens, 8), :] = jnp.zeros((8, half), jnp.bfloat16)
    sib_ref[pl.ds(tokens, 8), pl.ds(0, 128)] = pieces.astype(jnp.bfloat16)

    grad = kv_grad[...]
    tile = half // 4
    for t in range(4):
        rows = pl.ds(pl.multiple_of((1 - me) * half + t * tile, tile), tile)
        part = lax.dot_general(weight[rows, :], grad, LAST, preferred_element_type=jnp.float32)
        sib_ref[pl.ds(0, tokens), pl.ds(t * tile, tile)] = jnp.transpose(part.astype(jnp.bfloat16))
    att_out.wait()


def back_kernel(grad_ref, weight, own_ref):
    half = own_ref.shape[1]
    me = lax.axis_index("sec")
    grad = grad_ref[...]
    tile = half // 4
    for t in range(4):
        rows = pl.ds(pl.multiple_of(me * half + t * tile, tile), tile)
        own_ref[:, pl.ds(t * tile, tile)] = jnp.transpose(
            lax.dot_general(weight[rows, :], grad, LAST, preferred_element_type=jnp.float32)
        )


def chip_kernel(parts, own_ref, sib_ref, kept_ref, *big_refs):
    feats = kept_ref.shape[1]
    me, section = lax.axis_index("sec"), lax.axis_index("section")
    for k in range(parts):
        at = pl.multiple_of((section ^ section_step(me, k, parts)) * feats, feats)
        total = own_ref[:, pl.ds(at, feats)] + sib_ref[pl.ds(0, own_ref.shape[0]), pl.ds(at, feats)].astype(
            jnp.float32
        )
        if k == 0:
            kept_ref[...] = total
        else:
            big_refs[k - 1][...] = total.astype(jnp.bfloat16)


def gain_kernel(parts, row_ref, row_sib_ref, inv_ref, *refs):
    chunk_refs, total_refs, small_refs = refs[:parts], refs[parts : 2 * parts], refs[2 * parts :]
    feats = chunk_refs[0].shape[1]
    inv_rms = inv_ref[...]
    tokens = chunk_refs[0].shape[0]
    row = 0.0
    for ref in (row_ref, row_sib_ref):
        terms = ref[pl.ds(tokens, 8), pl.ds(0, 128)].astype(jnp.float32)
        row = row + ((terms[0:1, :] + terms[1:2, :]) + terms[2:3, :])
    for k in range(parts):
        normed = chunk_refs[k][...].astype(jnp.float32) * inv_rms
        total = total_refs[k][...].astype(jnp.float32)
        small_refs[k][:, pl.ds(0, feats)] = jnp.sum(total * normed, axis=0, keepdims=True)
        small_refs[k][:, pl.ds(feats, row.shape[1])] = row


def total_kernel(kept_ref, *refs):
    total = kept_ref[...]
    for ref in refs[:-1]:
        total = total + ref[...].astype(jnp.float32)
    refs[-1][...] = total


def last_kernel(parts, width, grad_ref, chunk_ref, inv_ref, gain_ref, *refs):
    small_refs, gain_refs, (enc_ref, row_ref, *gain_out) = refs[:parts], refs[parts:-3], refs[-3:]
    if not gain_refs:
        small_refs, (enc_ref, row_ref), gain_out = refs[:parts], refs[-2:], ()
    tokens, feats = chunk_ref.shape
    core = lax.axis_index("sec")
    rows = [ref[:, pl.ds(feats, tokens)] for ref in small_refs]
    row = tree_sum(
        [jnp.where(core == 0, rows[k], rows[reverse_bits(k, parts)]) for k in range(parts)]
    )
    row_ref[...] = row
    grad = grad_ref[...]
    inv_rms = inv_ref[...]
    at = pl.multiple_of((core * parts + lax.axis_index("section")) * feats, feats)
    gain = gain_ref[:, pl.ds(at, feats)]
    normed = chunk_ref[...].astype(jnp.float32) * inv_rms
    row_dot = jnp.transpose(jnp.broadcast_to(row, (128, tokens)))[:, 0:1]
    enc_ref[...] = (inv_rms * (gain * grad - normed * (row_dot / width))).astype(jnp.bfloat16)
    for ref in gain_out:
        ref[...] = tree_sum([g[...] for g in gain_refs])


def per_device(sizes, enc_states, norm_gain, kv_weight, queries, attn_cotangent, target_lengths):
    cores, parts, seqs = sizes
    rows = enc_states[0]
    tokens, feats = rows.shape
    weight = kv_weight[0]
    width = weight.shape[0]
    half = width // 2
    query, cot = queries[0, 0], attn_cotangent[0, 0]
    dec = query.shape[0]
    heads = query.shape[1] // HS
    gain = norm_gain.reshape(1, width)
    swap = [(0, 1), (1, 0)]

    def to_section(x, step):
        pairs = [
            (c * parts + i, c * parts + (i ^ section_step(c, step, parts)))
            for c in range(cores)
            for i in range(parts)
        ]
        return lax.ppermute(x, ("sec", "section"), pairs)

    def to_core(x):
        return lax.ppermute(x, "sec", swap)

    token = pl.pallas_call(
        first_kernel,
        out_shape=jax.ShapeDtypeStruct((8, 128), jnp.float32),
        out_specs=VMEM,
        compiler_params=pltpu.CompilerParams(vmem_limit_bytes=1 << 20),
        cost_estimate=pl.CostEstimate(flops=20_000_000_000, bytes_accessed=4096, transcendentals=0),
        name="first",
    )()
    flops = 2 * tokens * width * weight.shape[1]
    chunks = [rows]
    for k in range(1, parts):
        chunks.append(lax.optimization_barrier((to_section(rows, k), token))[0])
    first, second = range(1), range(1, parts)
    others = [to_core(chunks[k]) for k in first]
    product, square = pl.pallas_call(
        functools.partial(early_kernel, parts, first),
        out_shape=(
            jax.ShapeDtypeStruct((tokens, weight.shape[1]), jnp.float32),
            jax.ShapeDtypeStruct((tokens, 128), jnp.float32),
        ),
        in_specs=[VMEM] * (2 * len(first) + 2),
        out_specs=(VMEM, VMEM),
        compiler_params=pltpu.CompilerParams(vmem_limit_bytes=16 << 20),
        cost_estimate=pl.CostEstimate(
            flops=20_000_000_000, bytes_accessed=weight.size, transcendentals=0
        ),
        name="early",
    )(*[chunks[k] for k in first], *[others[k] for k in first], gain, weight)
    for k in second:
        chunks[k] = lax.optimization_barrier((chunks[k], square))[0]
        others.append(to_core(chunks[k]))
    att, sib, kv_grad, inv_rms = pl.pallas_call(
        functools.partial(main_kernel, parts, second, heads),
        out_shape=(
            jax.ShapeDtypeStruct(query.shape, jnp.bfloat16),
            jax.ShapeDtypeStruct((tokens + 8, half), jnp.bfloat16),
            jax.ShapeDtypeStruct((tokens, weight.shape[1]), jnp.bfloat16),
            jax.ShapeDtypeStruct((tokens, 1), jnp.float32),
        ),
        in_specs=[SMEM, ANY] + [VMEM] * (2 * len(second) + 6),
        out_specs=(ANY, VMEM, VMEM, VMEM),
        scratch_shapes=[
            pltpu.VMEM((tokens, weight.shape[1]), jnp.float32),
            pltpu.VMEM(query.shape, jnp.bfloat16),
            pltpu.SemaphoreType.DMA(()),
        ],
        compiler_params=pltpu.CompilerParams(vmem_limit_bytes=16 << 20),
        cost_estimate=pl.CostEstimate(
            flops=2 * flops, bytes_accessed=2 * weight.size, transcendentals=dec * tokens * heads
        ),
        name="main",
    )(
        target_lengths,
        token,
        *[chunks[k] for k in second],
        *[others[k] for k in second],
        product,
        square,
        gain,
        weight,
        query,
        cot,
    )
    own = pl.pallas_call(
        back_kernel,
        out_shape=jax.ShapeDtypeStruct((tokens, half), jnp.float32),
        in_specs=[VMEM, VMEM],
        out_specs=VMEM,
        compiler_params=pltpu.CompilerParams(vmem_limit_bytes=16 << 20),
        cost_estimate=pl.CostEstimate(
            flops=flops // 2, bytes_accessed=weight.size, transcendentals=0
        ),
        name="back",
    )(kv_grad, weight)
    sib_in = to_core(sib)

    kept, *big = pl.pallas_call(
        functools.partial(chip_kernel, parts),
        out_shape=(jax.ShapeDtypeStruct((tokens, feats), jnp.float32),)
        + (jax.ShapeDtypeStruct((tokens, feats), jnp.bfloat16),) * (parts - 1),
        in_specs=[VMEM] * 2,
        out_specs=(VMEM,) * parts,
        compiler_params=pltpu.CompilerParams(vmem_limit_bytes=16 << 20),
        cost_estimate=pl.CostEstimate(
            flops=2 * tokens * half, bytes_accessed=8 * tokens * half, transcendentals=0
        ),
        name="chip",
    )(own, sib_in)
    small = pl.pallas_call(
        functools.partial(gain_kernel, parts),
        out_shape=(jax.ShapeDtypeStruct((1, feats + tokens), jnp.float32),) * parts,
        in_specs=[VMEM] * (3 + 2 * parts),
        out_specs=(VMEM,) * parts,
        compiler_params=pltpu.CompilerParams(vmem_limit_bytes=16 << 20),
        cost_estimate=pl.CostEstimate(
            flops=20_000_000_000, bytes_accessed=8 * tokens * half, transcendentals=0
        ),
        name="gain",
    )(sib, sib_in, inv_rms, *chunks, kept, *big)

    big_in = [to_section(big[k - 1], k) for k in range(1, parts)]
    small_in = [small[0]] + [to_section(small[k], k) for k in range(1, parts)]
    gain_term = tree_sum([x[:, :feats] for x in small_in])
    direct = seqs <= 8 and (feats // seqs) % 128 == 0
    pieces = []
    if direct:
        piece = feats // seqs
        dp = lax.axis_index("dp")
        pieces = [lax.dynamic_slice_in_dim(gain_term, dp * piece, piece, 1)]
        for k in reversed(range(1, seqs)):
            send = lax.dynamic_slice_in_dim(gain_term, (dp ^ k) * piece, piece, 1)
            pieces.append(lax.ppermute(send, "dp", [(i, i ^ k) for i in range(seqs)]))
    total = pl.pallas_call(
        total_kernel,
        out_shape=jax.ShapeDtypeStruct((tokens, feats), jnp.float32),
        in_specs=[VMEM] * parts,
        out_specs=VMEM,
        compiler_params=pltpu.CompilerParams(vmem_limit_bytes=8 << 20),
        cost_estimate=pl.CostEstimate(flops=20_000_000_000, bytes_accessed=4096, transcendentals=0),
        name="total",
    )(kept, *big_in)
    enc_grad, row_dot, *gain_grad = pl.pallas_call(
        functools.partial(last_kernel, parts, width),
        out_shape=(
            jax.ShapeDtypeStruct((tokens, feats), jnp.bfloat16),
            jax.ShapeDtypeStruct((1, tokens), jnp.float32),
        )
        + ((jax.ShapeDtypeStruct(pieces[0].shape, jnp.float32),) if direct else ()),
        in_specs=[VMEM] * (4 + parts + len(pieces)),
        out_specs=(VMEM,) * (3 if direct else 2),
        compiler_params=pltpu.CompilerParams(vmem_limit_bytes=8 << 20),
        cost_estimate=pl.CostEstimate(
            flops=10 * tokens * feats, bytes_accessed=16 * tokens * feats, transcendentals=0
        ),
        name="last",
    )(total, rows, inv_rms, gain, *small_in, *pieces)
    if direct:
        gain_grad = gain_grad[0][0]
    else:
        gain_grad = lax.psum_scatter(gain_term[0], "dp", scatter_dimension=0, tiled=True)
    return (att[None, None], enc_grad[None], gain_grad, row_dot)


def solution(mesh):
    sizes = tuple(mesh.shape[a] for a in ("sec", "section", "dp"))
    placed = (
        P("dp", None, ("sec", "section")),
        P(),
        P("sec", None, "section"),
        P("sec", "dp", None, "section"),
        P("sec", "dp", None, "section"),
        P("dp"),
    )
    return jax.shard_map(
        functools.partial(per_device, sizes),
        mesh=mesh,
        in_specs=placed,
        out_specs=(
            P("sec", "dp", None, "section"),
            P("dp", None, ("sec", "section")),
            P(("sec", "section", "dp")),
            P("dp", None),
        ),
        check_vma=False,
    )
```

```python
import functools

import jax
import jax.numpy as jnp
from jax import lax
from jax.experimental import pallas as pl
from jax.experimental.pallas import tpu as pltpu
from jax.sharding import PartitionSpec as P

HS = 256
EPS = 1e-06
ROW_TERMS = 3
LAST = (((1,), (1,)), ((), ()))
FIRST = (((0,), (0,)), ((), ()))
VMEM = pl.BlockSpec(memory_space=pltpu.VMEM)
SMEM = pl.BlockSpec(memory_space=pltpu.SMEM)
ANY = pl.BlockSpec(memory_space=pl.ANY)


def reverse_bits(step, count):
    out, bit = 0, 1
    while bit < count:
        out = 2 * out + (1 if step & bit else 0)
        bit *= 2
    return out


def section_step(core, step, count):
    if isinstance(core, int):
        return reverse_bits(step, count) if core else step
    return jnp.where(core == 0, step, reverse_bits(step, count))


def tree_sum(terms):
    while len(terms) > 1:
        terms = [terms[i] + terms[i + 1] for i in range(0, len(terms), 2)]
    return terms[0]


def first_kernel(token_ref):
    token_ref[...] = jnp.zeros_like(token_ref)


def main_kernel(
    parts,
    heads,
    length_ref,
    token_ref,
    *refs,
):
    chunk_refs, refs = refs[: 2 * parts], refs[2 * parts :]
    (gain_ref, weight, query_ref, cot_ref) = refs[:4]
    (att_hbm, sib_ref, kv_grad, inv_ref) = refs[4:8]
    (kv, att_ref, sem) = refs[8:]
    tokens, feats = chunk_refs[0].shape
    width = weight.shape[0]
    half = width // 2
    me = lax.axis_index("sec")

    section = lax.axis_index("section")
    square = None
    for ref in chunk_refs:
        x = ref[...].astype(jnp.float32)
        x = x * x
        for i in range(0, feats, 128):
            square = x[:, i : i + 128] if square is None else square + x[:, i : i + 128]
    inv_rms = lax.rsqrt(jnp.sum(square, axis=1, keepdims=True) / width + EPS)
    inv_ref[...] = inv_rms
    for j, ref in enumerate(chunk_refs):
        owner = me if j < parts else 1 - me
        peer = section ^ section_step(owner, j % parts, parts)
        cols = pl.ds(pl.multiple_of((owner * parts + peer) * feats, feats), feats)
        normed = ref[...].astype(jnp.float32) * inv_rms
        memory = (normed * gain_ref[:, cols]).astype(jnp.bfloat16)
        product = jnp.dot(memory, weight[cols, :], preferred_element_type=jnp.float32)
        if j == 0:
            kv[...] = product
        else:
            kv[...] += product

    scale = HS ** (-0.5)
    live = lax.broadcasted_iota(jnp.int32, (query_ref.shape[0], HS), 0) < length_ref[0]
    row_part = None
    for h in range(heads):
        cols = pl.ds(h * HS, HS)
        key_cols, value_cols = pl.ds(2 * h * HS, HS), pl.ds((2 * h + 1) * HS, HS)
        key_full, value_full = kv[:, key_cols], kv[:, value_cols]
        key_rows, value_rows = key_full.astype(jnp.bfloat16), value_full.astype(jnp.bfloat16)
        query = query_ref[:, cols]
        cot = cot_ref[:, cols]
        masked = jnp.where(live, cot, jnp.zeros_like(cot))
        scores = lax.dot_general(key_rows, query, LAST, preferred_element_type=jnp.float32) * scale
        exponent = jnp.exp(scores)
        attention = exponent * (1.0 / jnp.sum(exponent, axis=0, keepdims=True))
        weights_b = attention.astype(jnp.bfloat16)
        att_ref[:, cols] = lax.dot_general(
            weights_b, value_rows, FIRST, preferred_element_type=jnp.float32
        ).astype(jnp.bfloat16)
        back = lax.dot_general(value_rows, masked, LAST, preferred_element_type=jnp.float32)
        mean = jnp.sum(attention * back, axis=0, keepdims=True)
        score_grad = (attention * (back - mean) * scale).astype(jnp.bfloat16)
        key_grad = jnp.dot(score_grad, query, preferred_element_type=jnp.float32)
        value_grad = jnp.dot(weights_b, masked, preferred_element_type=jnp.float32)
        key_grad, value_grad = key_grad.astype(jnp.bfloat16), value_grad.astype(jnp.bfloat16)
        kv_grad[:, key_cols] = key_grad
        kv_grad[:, value_cols] = value_grad
        here = jnp.sum(
            key_grad.astype(jnp.float32) * key_full + value_grad.astype(jnp.float32) * value_full,
            axis=1,
            keepdims=True,
        )
        row_part = here if row_part is None else row_part + here
    att_out = pltpu.make_async_copy(att_ref, att_hbm, sem)
    att_out.start()
    rest = jnp.transpose(jnp.broadcast_to(row_part, (tokens, 128)))[0:8, :]
    pieces = jnp.zeros_like(rest)
    place = lax.broadcasted_iota(jnp.int32, rest.shape, 0)
    for i in range(ROW_TERMS):
        term = rest.astype(jnp.bfloat16).astype(jnp.float32)
        pieces = jnp.where(place == i, term, pieces)
        rest = rest - term
    sib_ref[pl.ds(tokens, 8), :] = jnp.zeros((8, half), jnp.bfloat16)
    sib_ref[pl.ds(tokens, 8), pl.ds(0, 128)] = pieces.astype(jnp.bfloat16)

    grad = kv_grad[...]
    tile = half // 4
    for t in range(4):
        rows = pl.ds(pl.multiple_of((1 - me) * half + t * tile, tile), tile)
        part = lax.dot_general(weight[rows, :], grad, LAST, preferred_element_type=jnp.float32)
        sib_ref[pl.ds(0, tokens), pl.ds(t * tile, tile)] = jnp.transpose(part).astype(jnp.bfloat16)
    att_out.wait()


def back_kernel(grad_ref, weight, own_ref):
    half = own_ref.shape[1]
    me = lax.axis_index("sec")
    grad = grad_ref[...]
    tile = half // 8
    for t in range(8):
        rows = pl.ds(pl.multiple_of(me * half + t * tile, tile), tile)
        own_ref[:, pl.ds(t * tile, tile)] = jnp.transpose(
            lax.dot_general(weight[rows, :], grad, LAST, preferred_element_type=jnp.float32)
        )


def chip_kernel(parts, own_ref, sib_ref, kept_ref, *big_refs):
    feats = kept_ref.shape[1]
    me, section = lax.axis_index("sec"), lax.axis_index("section")
    for k in range(parts):
        at = pl.multiple_of((section ^ section_step(me, k, parts)) * feats, feats)
        total = own_ref[:, pl.ds(at, feats)] + sib_ref[pl.ds(0, own_ref.shape[0]), pl.ds(at, feats)].astype(
            jnp.float32
        )
        if k == 0:
            kept_ref[...] = total
        else:
            big_refs[k - 1][...] = total.astype(jnp.bfloat16)


def gain_kernel(parts, row_ref, row_sib_ref, inv_ref, *refs):
    chunk_refs, total_refs, small_refs = refs[:parts], refs[parts : 2 * parts], refs[2 * parts :]
    feats = chunk_refs[0].shape[1]
    inv_rms = inv_ref[...]
    tokens = chunk_refs[0].shape[0]
    row = 0.0
    for ref in (row_ref, row_sib_ref):
        terms = ref[pl.ds(tokens, 8), pl.ds(0, 128)].astype(jnp.float32)
        row = row + ((terms[0:1, :] + terms[1:2, :]) + terms[2:3, :])
    for k in range(parts):
        normed = chunk_refs[k][...].astype(jnp.float32) * inv_rms
        total = total_refs[k][...].astype(jnp.float32)
        small_refs[k][:, pl.ds(0, feats)] = jnp.sum(total * normed, axis=0, keepdims=True)
        small_refs[k][:, pl.ds(feats, row.shape[1])] = row


def total_kernel(kept_ref, *refs):
    total = kept_ref[...]
    for ref in refs[:-1]:
        total = total + ref[...].astype(jnp.float32)
    refs[-1][...] = total


def last_kernel(parts, width, grad_ref, chunk_ref, inv_ref, gain_ref, *refs):
    small_refs, gain_refs, (enc_ref, row_ref, *gain_out) = refs[:parts], refs[parts:-3], refs[-3:]
    if not gain_refs:
        small_refs, (enc_ref, row_ref), gain_out = refs[:parts], refs[-2:], ()
    tokens, feats = chunk_ref.shape
    core = lax.axis_index("sec")
    rows = [ref[:, pl.ds(feats, tokens)] for ref in small_refs]
    row = tree_sum(
        [jnp.where(core == 0, rows[k], rows[reverse_bits(k, parts)]) for k in range(parts)]
    )
    row_ref[...] = row
    grad = grad_ref[...]
    inv_rms = inv_ref[...]
    at = pl.multiple_of((core * parts + lax.axis_index("section")) * feats, feats)
    gain = gain_ref[:, pl.ds(at, feats)]
    normed = chunk_ref[...].astype(jnp.float32) * inv_rms
    row_dot = jnp.transpose(jnp.broadcast_to(row, (128, tokens)))[:, 0:1]
    enc_ref[...] = (inv_rms * (gain * grad - normed * (row_dot / width))).astype(jnp.bfloat16)
    for ref in gain_out:
        ref[...] = tree_sum([g[...] for g in gain_refs])


def per_device(sizes, enc_states, norm_gain, kv_weight, queries, attn_cotangent, target_lengths):
    cores, parts, seqs = sizes
    rows = enc_states[0]
    tokens, feats = rows.shape
    weight = kv_weight[0]
    width = weight.shape[0]
    half = width // 2
    query, cot = queries[0, 0], attn_cotangent[0, 0]
    dec = query.shape[0]
    heads = query.shape[1] // HS
    gain = norm_gain.reshape(1, width)
    swap = [(0, 1), (1, 0)]

    def to_section(x, step):
        pairs = [
            (c * parts + i, c * parts + (i ^ section_step(c, step, parts)))
            for c in range(cores)
            for i in range(parts)
        ]
        return lax.ppermute(x, ("sec", "section"), pairs)

    def to_core(x):
        return lax.ppermute(x, "sec", swap)

    token = pl.pallas_call(
        first_kernel,
        out_shape=jax.ShapeDtypeStruct((8, 128), jnp.float32),
        out_specs=VMEM,
        compiler_params=pltpu.CompilerParams(vmem_limit_bytes=1 << 20),
        cost_estimate=pl.CostEstimate(flops=20_000_000_000, bytes_accessed=4096, transcendentals=0),
        name="first",
    )()
    flops = 2 * tokens * width * weight.shape[1]
    chunks = [rows]
    for k in range(1, parts):
        chunks.append(lax.optimization_barrier((to_section(rows, k), token))[0])
    others = [to_core(c) for c in chunks]
    att, sib, kv_grad, inv_rms = pl.pallas_call(
        functools.partial(main_kernel, parts, heads),
        out_shape=(
            jax.ShapeDtypeStruct(query.shape, jnp.bfloat16),
            jax.ShapeDtypeStruct((tokens + 8, half), jnp.bfloat16),
            jax.ShapeDtypeStruct((tokens, weight.shape[1]), jnp.bfloat16),
            jax.ShapeDtypeStruct((tokens, 1), jnp.float32),
        ),
        in_specs=[SMEM, ANY] + [VMEM] * (2 * parts + 4),
        out_specs=(ANY, VMEM, VMEM, VMEM),
        scratch_shapes=[
            pltpu.VMEM((tokens, weight.shape[1]), jnp.float32),
            pltpu.VMEM(query.shape, jnp.bfloat16),
            pltpu.SemaphoreType.DMA(()),
        ],
        compiler_params=pltpu.CompilerParams(vmem_limit_bytes=16 << 20),
        cost_estimate=pl.CostEstimate(
            flops=2 * flops, bytes_accessed=2 * weight.size, transcendentals=dec * tokens * heads
        ),
        name="main",
    )(
        target_lengths,
        token,
        *chunks,
        *others,
        gain,
        weight,
        query,
        cot,
    )
    own = pl.pallas_call(
        back_kernel,
        out_shape=jax.ShapeDtypeStruct((tokens, half), jnp.float32),
        in_specs=[VMEM, VMEM],
        out_specs=VMEM,
        compiler_params=pltpu.CompilerParams(vmem_limit_bytes=16 << 20),
        cost_estimate=pl.CostEstimate(
            flops=flops // 2, bytes_accessed=weight.size, transcendentals=0
        ),
        name="back",
    )(kv_grad, weight)
    sib_in = to_core(sib)

    kept, *big = pl.pallas_call(
        functools.partial(chip_kernel, parts),
        out_shape=(jax.ShapeDtypeStruct((tokens, feats), jnp.float32),)
        + (jax.ShapeDtypeStruct((tokens, feats), jnp.bfloat16),) * (parts - 1),
        in_specs=[VMEM] * 2,
        out_specs=(VMEM,) * parts,
        compiler_params=pltpu.CompilerParams(vmem_limit_bytes=16 << 20),
        cost_estimate=pl.CostEstimate(
            flops=2 * tokens * half, bytes_accessed=8 * tokens * half, transcendentals=0
        ),
        name="chip",
    )(own, sib_in)
    small = pl.pallas_call(
        functools.partial(gain_kernel, parts),
        out_shape=(jax.ShapeDtypeStruct((1, feats + tokens), jnp.float32),) * parts,
        in_specs=[VMEM] * (3 + 2 * parts),
        out_specs=(VMEM,) * parts,
        compiler_params=pltpu.CompilerParams(vmem_limit_bytes=16 << 20),
        cost_estimate=pl.CostEstimate(
            flops=20_000_000_000, bytes_accessed=8 * tokens * half, transcendentals=0
        ),
        name="gain",
    )(sib, sib_in, inv_rms, *chunks, kept, *big)

    big_in = [to_section(big[k - 1], k) for k in range(1, parts)]
    small_in = [small[0]] + [to_section(small[k], k) for k in range(1, parts)]
    gain_term = tree_sum([x[:, :feats] for x in small_in])
    direct = seqs <= 8 and (feats // seqs) % 128 == 0
    pieces = []
    if direct:
        piece = feats // seqs
        dp = lax.axis_index("dp")
        pieces = [lax.dynamic_slice_in_dim(gain_term, dp * piece, piece, 1)]
        for k in reversed(range(1, seqs)):
            send = lax.dynamic_slice_in_dim(gain_term, (dp ^ k) * piece, piece, 1)
            pieces.append(lax.ppermute(send, "dp", [(i, i ^ k) for i in range(seqs)]))
    total = pl.pallas_call(
        total_kernel,
        out_shape=jax.ShapeDtypeStruct((tokens, feats), jnp.float32),
        in_specs=[VMEM] * parts,
        out_specs=VMEM,
        compiler_params=pltpu.CompilerParams(vmem_limit_bytes=8 << 20),
        cost_estimate=pl.CostEstimate(flops=20_000_000_000, bytes_accessed=4096, transcendentals=0),
        name="total",
    )(kept, *big_in)
    enc_grad, row_dot, *gain_grad = pl.pallas_call(
        functools.partial(last_kernel, parts, width),
        out_shape=(
            jax.ShapeDtypeStruct((tokens, feats), jnp.bfloat16),
            jax.ShapeDtypeStruct((1, tokens), jnp.float32),
        )
        + ((jax.ShapeDtypeStruct(pieces[0].shape, jnp.float32),) if direct else ()),
        in_specs=[VMEM] * (4 + parts + len(pieces)),
        out_specs=(VMEM,) * (3 if direct else 2),
        compiler_params=pltpu.CompilerParams(vmem_limit_bytes=8 << 20),
        cost_estimate=pl.CostEstimate(
            flops=10 * tokens * feats, bytes_accessed=16 * tokens * feats, transcendentals=0
        ),
        name="last",
    )(total, rows, inv_rms, gain, *small_in, *pieces)
    if direct:
        gain_grad = gain_grad[0][0]
    else:
        gain_grad = lax.psum_scatter(gain_term[0], "dp", scatter_dimension=0, tiled=True)
    return (att[None, None], enc_grad[None], gain_grad, row_dot)


def solution(mesh):
    sizes = tuple(mesh.shape[a] for a in ("sec", "section", "dp"))
    placed = (
        P("dp", None, ("sec", "section")),
        P(),
        P("sec", None, "section"),
        P("sec", "dp", None, "section"),
        P("sec", "dp", None, "section"),
        P("dp"),
    )
    return jax.shard_map(
        functools.partial(per_device, sizes),
        mesh=mesh,
        in_specs=placed,
        out_specs=(
            P("sec", "dp", None, "section"),
            P("dp", None, ("sec", "section")),
            P(("sec", "section", "dp")),
            P("dp", None),
        ),
        check_vma=False,
    )
```

```python
import functools

import jax
import jax.numpy as jnp
from jax import lax
from jax.experimental import pallas as pl
from jax.experimental.pallas import tpu as pltpu
from jax.sharding import PartitionSpec as P

HS = 256
EPS = 1e-06
ROW_TERMS = 3
LAST = (((1,), (1,)), ((), ()))
FIRST = (((0,), (0,)), ((), ()))
VMEM = pl.BlockSpec(memory_space=pltpu.VMEM)
SMEM = pl.BlockSpec(memory_space=pltpu.SMEM)
ANY = pl.BlockSpec(memory_space=pl.ANY)


def reverse_bits(step, count):
    out, bit = 0, 1
    while bit < count:
        out = 2 * out + (1 if step & bit else 0)
        bit *= 2
    return out


def section_step(core, step, count):
    if isinstance(core, int):
        return reverse_bits(step, count) if core else step
    return jnp.where(core == 0, step, reverse_bits(step, count))


def tree_sum(terms):
    while len(terms) > 1:
        terms = [terms[i] + terms[i + 1] for i in range(0, len(terms), 2)]
    return terms[0]


def first_kernel(token_ref):
    token_ref[...] = jnp.zeros_like(token_ref)


def main_kernel(
    parts,
    heads,
    length_ref,
    token_ref,
    *refs,
):
    chunk_refs, refs = refs[: 2 * parts], refs[2 * parts :]
    (gain_ref, weight, query_ref, cot_ref) = refs[:4]
    (att_hbm, sib_ref, kv_grad, inv_ref) = refs[4:8]
    (kv, att_ref, sem) = refs[8:]
    tokens, feats = chunk_refs[0].shape
    width = weight.shape[0]
    half = width // 2
    me = lax.axis_index("sec")

    section = lax.axis_index("section")
    square = None
    for ref in chunk_refs:
        x = ref[...].astype(jnp.float32)
        x = x * x
        for i in range(0, feats, 128):
            square = x[:, i : i + 128] if square is None else square + x[:, i : i + 128]
    inv_rms = lax.rsqrt(jnp.sum(square, axis=1, keepdims=True) / width + EPS)
    inv_ref[...] = inv_rms
    for j, ref in enumerate(chunk_refs):
        owner = me if j < parts else 1 - me
        peer = section ^ section_step(owner, j % parts, parts)
        cols = pl.ds(pl.multiple_of((owner * parts + peer) * feats, feats), feats)
        normed = ref[...].astype(jnp.float32) * inv_rms
        memory = (normed * gain_ref[:, cols]).astype(jnp.bfloat16)
        product = jnp.dot(memory, weight[cols, :], preferred_element_type=jnp.float32)
        if j == 0:
            kv[...] = product
        else:
            kv[...] += product

    scale = HS ** (-0.5)
    live = lax.broadcasted_iota(jnp.int32, (query_ref.shape[0], HS), 0) < length_ref[0]
    row_part = None
    for h in range(heads):
        cols = pl.ds(h * HS, HS)
        key_cols, value_cols = pl.ds(2 * h * HS, HS), pl.ds((2 * h + 1) * HS, HS)
        key_full, value_full = kv[:, key_cols], kv[:, value_cols]
        key_rows, value_rows = key_full.astype(jnp.bfloat16), value_full.astype(jnp.bfloat16)
        query = query_ref[:, cols]
        cot = cot_ref[:, cols]
        masked = jnp.where(live, cot, jnp.zeros_like(cot))
        scores = lax.dot_general(key_rows, query, LAST, preferred_element_type=jnp.float32) * scale
        exponent = jnp.exp(scores)
        attention = exponent / jnp.sum(exponent, axis=0, keepdims=True)
        weights_b = attention.astype(jnp.bfloat16)
        att_ref[:, cols] = lax.dot_general(
            weights_b, value_rows, FIRST, preferred_element_type=jnp.float32
        ).astype(jnp.bfloat16)
        back = lax.dot_general(value_rows, masked, LAST, preferred_element_type=jnp.float32)
        mean = jnp.sum(attention * back, axis=0, keepdims=True)
        score_grad = (attention * (back - mean) * scale).astype(jnp.bfloat16)
        key_grad = jnp.dot(score_grad, query, preferred_element_type=jnp.float32)
        value_grad = jnp.dot(weights_b, masked, preferred_element_type=jnp.float32)
        key_grad, value_grad = key_grad.astype(jnp.bfloat16), value_grad.astype(jnp.bfloat16)
        kv_grad[:, key_cols] = key_grad
        kv_grad[:, value_cols] = value_grad
        here = jnp.sum(
            key_grad.astype(jnp.float32) * key_full + value_grad.astype(jnp.float32) * value_full,
            axis=1,
            keepdims=True,
        )
        row_part = here if row_part is None else row_part + here
    att_out = pltpu.make_async_copy(att_ref, att_hbm, sem)
    att_out.start()
    rest = jnp.transpose(jnp.broadcast_to(row_part, (tokens, 128)))[0:8, :]
    pieces = jnp.zeros_like(rest)
    place = lax.broadcasted_iota(jnp.int32, rest.shape, 0)
    for i in range(ROW_TERMS):
        term = rest.astype(jnp.bfloat16).astype(jnp.float32)
        pieces = jnp.where(place == i, term, pieces)
        rest = rest - term
    sib_ref[pl.ds(tokens, 8), :] = jnp.zeros((8, half), jnp.bfloat16)
    sib_ref[pl.ds(tokens, 8), pl.ds(0, 128)] = pieces.astype(jnp.bfloat16)

    grad = kv_grad[...]
    tile = half // 4
    for t in range(4):
        rows = pl.ds(pl.multiple_of((1 - me) * half + t * tile, tile), tile)
        part = lax.dot_general(weight[rows, :], grad, LAST, preferred_element_type=jnp.float32)
        sib_ref[pl.ds(0, tokens), pl.ds(t * tile, tile)] = jnp.transpose(part).astype(jnp.bfloat16)
    att_out.wait()


def back_kernel(grad_ref, weight, own_ref):
    half = own_ref.shape[1]
    me = lax.axis_index("sec")
    grad = grad_ref[...]
    tile = half // 8
    for t in range(8):
        rows = pl.ds(pl.multiple_of(me * half + t * tile, tile), tile)
        own_ref[:, pl.ds(t * tile, tile)] = jnp.transpose(
            lax.dot_general(weight[rows, :], grad, LAST, preferred_element_type=jnp.float32)
        )


def chip_kernel(parts, own_ref, sib_ref, kept_ref, *big_refs):
    feats = kept_ref.shape[1]
    me, section = lax.axis_index("sec"), lax.axis_index("section")
    for k in range(parts):
        at = pl.multiple_of((section ^ section_step(me, k, parts)) * feats, feats)
        total = own_ref[:, pl.ds(at, feats)] + sib_ref[pl.ds(0, own_ref.shape[0]), pl.ds(at, feats)].astype(
            jnp.float32
        )
        if k == 0:
            kept_ref[...] = total
        else:
            big_refs[k - 1][...] = total.astype(jnp.bfloat16)


def gain_kernel(parts, row_ref, row_sib_ref, inv_ref, *refs):
    chunk_refs, total_refs, small_refs = refs[:parts], refs[parts : 2 * parts], refs[2 * parts :]
    feats = chunk_refs[0].shape[1]
    inv_rms = inv_ref[...]
    tokens = chunk_refs[0].shape[0]
    row = 0.0
    for ref in (row_ref, row_sib_ref):
        terms = ref[pl.ds(tokens, 8), pl.ds(0, 128)].astype(jnp.float32)
        row = row + ((terms[0:1, :] + terms[1:2, :]) + terms[2:3, :])
    for k in range(parts):
        normed = chunk_refs[k][...].astype(jnp.float32) * inv_rms
        total = total_refs[k][...].astype(jnp.float32)
        small_refs[k][:, pl.ds(0, feats)] = jnp.sum(total * normed, axis=0, keepdims=True)
        small_refs[k][:, pl.ds(feats, row.shape[1])] = row


def last_kernel(parts, width, kept_ref, *refs):
    big_refs, (chunk_ref, inv_ref, gain_ref) = refs[: parts - 1], refs[parts - 1 : parts + 2]
    small_refs, (enc_ref, row_ref) = refs[parts + 2 : 2 * parts + 2], refs[2 * parts + 2 :]
    tokens, feats = chunk_ref.shape
    core = lax.axis_index("sec")
    rows = [ref[:, pl.ds(feats, tokens)] for ref in small_refs]
    row = tree_sum(
        [jnp.where(core == 0, rows[k], rows[reverse_bits(k, parts)]) for k in range(parts)]
    )
    row_ref[...] = row
    grad = kept_ref[...]
    for ref in big_refs:
        grad = grad + ref[...].astype(jnp.float32)
    inv_rms = inv_ref[...]
    at = pl.multiple_of((core * parts + lax.axis_index("section")) * feats, feats)
    gain = gain_ref[:, pl.ds(at, feats)]
    normed = chunk_ref[...].astype(jnp.float32) * inv_rms
    row_dot = jnp.transpose(jnp.broadcast_to(row, (128, tokens)))[:, 0:1]
    enc_ref[...] = (inv_rms * (gain * grad - normed * (row_dot / width))).astype(jnp.bfloat16)


def per_device(sizes, enc_states, norm_gain, kv_weight, queries, attn_cotangent, target_lengths):
    cores, parts, seqs = sizes
    rows = enc_states[0]
    tokens, feats = rows.shape
    weight = kv_weight[0]
    width = weight.shape[0]
    half = width // 2
    query, cot = queries[0, 0], attn_cotangent[0, 0]
    dec = query.shape[0]
    heads = query.shape[1] // HS
    gain = norm_gain.reshape(1, width)
    swap = [(0, 1), (1, 0)]

    def to_section(x, step):
        pairs = [
            (c * parts + i, c * parts + (i ^ section_step(c, step, parts)))
            for c in range(cores)
            for i in range(parts)
        ]
        return lax.ppermute(x, ("sec", "section"), pairs)

    def to_core(x):
        return lax.ppermute(x, "sec", swap)

    token = pl.pallas_call(
        first_kernel,
        out_shape=jax.ShapeDtypeStruct((8, 128), jnp.float32),
        out_specs=VMEM,
        compiler_params=pltpu.CompilerParams(vmem_limit_bytes=1 << 20),
        cost_estimate=pl.CostEstimate(flops=20_000_000_000, bytes_accessed=4096, transcendentals=0),
        name="first",
    )()
    flops = 2 * tokens * width * weight.shape[1]
    chunks = [rows]
    for k in range(1, parts):
        chunks.append(lax.optimization_barrier((to_section(rows, k), token))[0])
    others = [to_core(c) for c in chunks]
    att, sib, kv_grad, inv_rms = pl.pallas_call(
        functools.partial(main_kernel, parts, heads),
        out_shape=(
            jax.ShapeDtypeStruct(query.shape, jnp.bfloat16),
            jax.ShapeDtypeStruct((tokens + 8, half), jnp.bfloat16),
            jax.ShapeDtypeStruct((tokens, weight.shape[1]), jnp.bfloat16),
            jax.ShapeDtypeStruct((tokens, 1), jnp.float32),
        ),
        in_specs=[SMEM, ANY] + [VMEM] * (2 * parts + 4),
        out_specs=(ANY, VMEM, VMEM, VMEM),
        scratch_shapes=[
            pltpu.VMEM((tokens, weight.shape[1]), jnp.float32),
            pltpu.VMEM(query.shape, jnp.bfloat16),
            pltpu.SemaphoreType.DMA(()),
        ],
        compiler_params=pltpu.CompilerParams(vmem_limit_bytes=16 << 20),
        cost_estimate=pl.CostEstimate(
            flops=2 * flops, bytes_accessed=2 * weight.size, transcendentals=dec * tokens * heads
        ),
        name="main",
    )(
        target_lengths,
        token,
        *chunks,
        *others,
        gain,
        weight,
        query,
        cot,
    )
    own = pl.pallas_call(
        back_kernel,
        out_shape=jax.ShapeDtypeStruct((tokens, half), jnp.float32),
        in_specs=[VMEM, VMEM],
        out_specs=VMEM,
        compiler_params=pltpu.CompilerParams(vmem_limit_bytes=16 << 20),
        cost_estimate=pl.CostEstimate(
            flops=flops // 2, bytes_accessed=weight.size, transcendentals=0
        ),
        name="back",
    )(kv_grad, weight)
    sib_in = to_core(sib)

    kept, *big = pl.pallas_call(
        functools.partial(chip_kernel, parts),
        out_shape=(jax.ShapeDtypeStruct((tokens, feats), jnp.float32),)
        + (jax.ShapeDtypeStruct((tokens, feats), jnp.bfloat16),) * (parts - 1),
        in_specs=[VMEM] * 2,
        out_specs=(VMEM,) * parts,
        compiler_params=pltpu.CompilerParams(vmem_limit_bytes=16 << 20),
        cost_estimate=pl.CostEstimate(
            flops=2 * tokens * half, bytes_accessed=8 * tokens * half, transcendentals=0
        ),
        name="chip",
    )(own, sib_in)
    small = pl.pallas_call(
        functools.partial(gain_kernel, parts),
        out_shape=(jax.ShapeDtypeStruct((1, feats + tokens), jnp.float32),) * parts,
        in_specs=[VMEM] * (3 + 2 * parts),
        out_specs=(VMEM,) * parts,
        compiler_params=pltpu.CompilerParams(vmem_limit_bytes=16 << 20),
        cost_estimate=pl.CostEstimate(
            flops=20_000_000_000, bytes_accessed=8 * tokens * half, transcendentals=0
        ),
        name="gain",
    )(sib, sib_in, inv_rms, *chunks, kept, *big)

    big_in = [to_section(big[k - 1], k) for k in range(1, parts)]
    small_in = [small[0]] + [to_section(small[k], k) for k in range(1, parts)]
    gain_term = tree_sum([x[:, :feats] for x in small_in])
    direct = seqs <= 8 and (feats // seqs) % 128 == 0
    pieces = []
    if direct:
        piece = feats // seqs
        dp = lax.axis_index("dp")
        pieces = [lax.dynamic_slice_in_dim(gain_term, dp * piece, piece, 1)]
        for k in reversed(range(1, seqs)):
            send = lax.dynamic_slice_in_dim(gain_term, (dp ^ k) * piece, piece, 1)
            pieces.append(lax.ppermute(send, "dp", [(i, i ^ k) for i in range(seqs)]))
    enc_grad, row_dot = pl.pallas_call(
        functools.partial(last_kernel, parts, width),
        out_shape=(
            jax.ShapeDtypeStruct((tokens, feats), jnp.bfloat16),
            jax.ShapeDtypeStruct((1, tokens), jnp.float32),
        ),
        in_specs=[VMEM] * (2 * parts + 3),
        out_specs=(VMEM, VMEM),
        compiler_params=pltpu.CompilerParams(vmem_limit_bytes=8 << 20),
        cost_estimate=pl.CostEstimate(flops=20_000_000_000, bytes_accessed=4096, transcendentals=0),
        name="last",
    )(kept, *big_in, rows, inv_rms, gain, *small_in)
    if direct:
        enc_grad, pieces[0] = lax.optimization_barrier((enc_grad, pieces[0]))
        gain_grad = tree_sum(pieces)[0]
    else:
        gain_grad = lax.psum_scatter(gain_term[0], "dp", scatter_dimension=0, tiled=True)
    return (att[None, None], enc_grad[None], gain_grad, row_dot)


def solution(mesh):
    sizes = tuple(mesh.shape[a] for a in ("sec", "section", "dp"))
    placed = (
        P("dp", None, ("sec", "section")),
        P(),
        P("sec", None, "section"),
        P("sec", "dp", None, "section"),
        P("sec", "dp", None, "section"),
        P("dp"),
    )
    return jax.shard_map(
        functools.partial(per_device, sizes),
        mesh=mesh,
        in_specs=placed,
        out_specs=(
            P("sec", "dp", None, "section"),
            P("dp", None, ("sec", "section")),
            P(("sec", "section", "dp")),
            P("dp", None),
        ),
        check_vma=False,
    )
```

```python
import functools

import jax
import jax.numpy as jnp
from jax import lax
from jax.experimental import pallas as pl
from jax.experimental.pallas import tpu as pltpu
from jax.sharding import PartitionSpec as P

HS = 256
EPS = 1e-06
ROW_TERMS = 3
LAST = (((1,), (1,)), ((), ()))
FIRST = (((0,), (0,)), ((), ()))
VMEM = pl.BlockSpec(memory_space=pltpu.VMEM)
SMEM = pl.BlockSpec(memory_space=pltpu.SMEM)
ANY = pl.BlockSpec(memory_space=pl.ANY)


def reverse_bits(step, count):
    out, bit = 0, 1
    while bit < count:
        out = 2 * out + (1 if step & bit else 0)
        bit *= 2
    return out


def section_step(core, step, count):
    if isinstance(core, int):
        return reverse_bits(step, count) if core else step
    return jnp.where(core == 0, step, reverse_bits(step, count))


def tree_sum(terms):
    while len(terms) > 1:
        terms = [terms[i] + terms[i + 1] for i in range(0, len(terms), 2)]
    return terms[0]


def first_kernel(token_ref):
    token_ref[...] = jnp.zeros_like(token_ref)


def main_kernel(
    parts,
    heads,
    length_ref,
    token_ref,
    *refs,
):
    chunk_refs, refs = refs[: 2 * parts], refs[2 * parts :]
    (gain_ref, weight, query_ref, cot_ref) = refs[:4]
    (att_hbm, sib_ref, kv_grad, inv_ref) = refs[4:8]
    (kv, att_ref, sem) = refs[8:]
    tokens, feats = chunk_refs[0].shape
    width = weight.shape[0]
    half = width // 2
    me = lax.axis_index("sec")

    section = lax.axis_index("section")
    square = None
    for ref in chunk_refs:
        x = ref[...].astype(jnp.float32)
        x = x * x
        for i in range(0, feats, 128):
            square = x[:, i : i + 128] if square is None else square + x[:, i : i + 128]
    inv_rms = lax.rsqrt(jnp.sum(square, axis=1, keepdims=True) / width + EPS)
    inv_ref[...] = inv_rms
    for j, ref in enumerate(chunk_refs):
        owner = me if j < parts else 1 - me
        peer = section ^ section_step(owner, j % parts, parts)
        cols = pl.ds(pl.multiple_of((owner * parts + peer) * feats, feats), feats)
        normed = ref[...].astype(jnp.float32) * inv_rms
        memory = (normed * gain_ref[:, cols]).astype(jnp.bfloat16)
        product = jnp.dot(memory, weight[cols, :], preferred_element_type=jnp.float32)
        if j == 0:
            kv[...] = product
        else:
            kv[...] += product

    scale = HS ** (-0.5)
    live = lax.broadcasted_iota(jnp.int32, (query_ref.shape[0], HS), 0) < length_ref[0]
    every = range(heads)
    cols = [pl.ds(h * HS, HS) for h in every]
    key_cols = [pl.ds(2 * h * HS, HS) for h in every]
    value_cols = [pl.ds((2 * h + 1) * HS, HS) for h in every]
    key_rows = [kv[:, c].astype(jnp.bfloat16) for c in key_cols]
    value_rows = [kv[:, c].astype(jnp.bfloat16) for c in value_cols]
    query = [query_ref[:, c] for c in cols]
    masked = [jnp.where(live, cot_ref[:, c], jnp.zeros((), jnp.bfloat16)) for c in cols]
    scores = [
        lax.dot_general(key_rows[h], query[h], LAST, preferred_element_type=jnp.float32) * scale
        for h in every
    ]
    back = [
        lax.dot_general(value_rows[h], masked[h], LAST, preferred_element_type=jnp.float32)
        for h in every
    ]
    exponent = [jnp.exp(x) for x in scores]
    attention = [x / jnp.sum(x, axis=0, keepdims=True) for x in exponent]
    weights_b = [x.astype(jnp.bfloat16) for x in attention]
    mean = [jnp.sum(attention[h] * back[h], axis=0, keepdims=True) for h in every]
    score_grad = [
        (attention[h] * (back[h] - mean[h]) * scale).astype(jnp.bfloat16) for h in every
    ]
    for h in every:
        att_ref[:, cols[h]] = lax.dot_general(
            weights_b[h], value_rows[h], FIRST, preferred_element_type=jnp.float32
        ).astype(jnp.bfloat16)
    key_grad = [
        jnp.dot(score_grad[h], query[h], preferred_element_type=jnp.float32).astype(jnp.bfloat16)
        for h in every
    ]
    value_grad = [
        jnp.dot(weights_b[h], masked[h], preferred_element_type=jnp.float32).astype(jnp.bfloat16)
        for h in every
    ]
    row_part = None
    for h in every:
        kv_grad[:, key_cols[h]] = key_grad[h]
        kv_grad[:, value_cols[h]] = value_grad[h]
        here = key_grad[h].astype(jnp.float32) * kv[:, key_cols[h]]
        here = here + value_grad[h].astype(jnp.float32) * kv[:, value_cols[h]]
        row_part = here if row_part is None else row_part + here
    row_part = jnp.sum(row_part, axis=1, keepdims=True)
    att_out = pltpu.make_async_copy(att_ref, att_hbm, sem)
    att_out.start()
    rest = jnp.transpose(jnp.broadcast_to(row_part, (tokens, 128)))[0:8, :]
    pieces = jnp.zeros_like(rest)
    place = lax.broadcasted_iota(jnp.int32, rest.shape, 0)
    for i in range(ROW_TERMS):
        term = rest.astype(jnp.bfloat16).astype(jnp.float32)
        pieces = jnp.where(place == i, term, pieces)
        rest = rest - term
    sib_ref[pl.ds(tokens, 8), :] = jnp.zeros((8, half), jnp.bfloat16)
    sib_ref[pl.ds(tokens, 8), pl.ds(0, 128)] = pieces.astype(jnp.bfloat16)

    grad = kv_grad[...]
    tile = half // 4
    for t in range(4):
        rows = pl.ds(pl.multiple_of((1 - me) * half + t * tile, tile), tile)
        part = lax.dot_general(weight[rows, :], grad, LAST, preferred_element_type=jnp.float32)
        sib_ref[pl.ds(0, tokens), pl.ds(t * tile, tile)] = jnp.transpose(part).astype(jnp.bfloat16)
    att_out.wait()


def back_kernel(grad_ref, weight, own_ref):
    half = own_ref.shape[1]
    me = lax.axis_index("sec")
    grad = grad_ref[...]
    tile = half // 8
    for t in range(8):
        rows = pl.ds(pl.multiple_of(me * half + t * tile, tile), tile)
        own_ref[:, pl.ds(t * tile, tile)] = jnp.transpose(
            lax.dot_general(weight[rows, :], grad, LAST, preferred_element_type=jnp.float32)
        )


def chip_kernel(parts, own_ref, sib_ref, kept_ref, *big_refs):
    feats = kept_ref.shape[1]
    me, section = lax.axis_index("sec"), lax.axis_index("section")
    for k in range(parts):
        at = pl.multiple_of((section ^ section_step(me, k, parts)) * feats, feats)
        total = own_ref[:, pl.ds(at, feats)] + sib_ref[pl.ds(0, own_ref.shape[0]), pl.ds(at, feats)].astype(
            jnp.float32
        )
        if k == 0:
            kept_ref[...] = total
        else:
            big_refs[k - 1][...] = total.astype(jnp.bfloat16)


def gain_kernel(parts, row_ref, row_sib_ref, inv_ref, *refs):
    chunk_refs, total_refs, small_refs = refs[:parts], refs[parts : 2 * parts], refs[2 * parts :]
    feats = chunk_refs[0].shape[1]
    inv_rms = inv_ref[...]
    tokens = chunk_refs[0].shape[0]
    row = 0.0
    for ref in (row_ref, row_sib_ref):
        terms = ref[pl.ds(tokens, 8), pl.ds(0, 128)].astype(jnp.float32)
        row = row + ((terms[0:1, :] + terms[1:2, :]) + terms[2:3, :])
    for k in range(parts):
        normed = chunk_refs[k][...].astype(jnp.float32) * inv_rms
        total = total_refs[k][...].astype(jnp.float32)
        small_refs[k][:, pl.ds(0, feats)] = jnp.sum(total * normed, axis=0, keepdims=True)
        small_refs[k][:, pl.ds(feats, row.shape[1])] = row


def last_kernel(parts, width, kept_ref, *refs):
    big_refs, (chunk_ref, inv_ref, gain_ref) = refs[: parts - 1], refs[parts - 1 : parts + 2]
    small_refs, (enc_ref, row_ref) = refs[parts + 2 : 2 * parts + 2], refs[2 * parts + 2 :]
    tokens, feats = chunk_ref.shape
    core = lax.axis_index("sec")
    rows = [ref[:, pl.ds(feats, tokens)] for ref in small_refs]
    row = tree_sum(
        [jnp.where(core == 0, rows[k], rows[reverse_bits(k, parts)]) for k in range(parts)]
    )
    row_ref[...] = row
    grad = kept_ref[...]
    for ref in big_refs:
        grad = grad + ref[...].astype(jnp.float32)
    inv_rms = inv_ref[...]
    at = pl.multiple_of((core * parts + lax.axis_index("section")) * feats, feats)
    gain = gain_ref[:, pl.ds(at, feats)]
    normed = chunk_ref[...].astype(jnp.float32) * inv_rms
    row_dot = jnp.transpose(jnp.broadcast_to(row, (128, tokens)))[:, 0:1]
    enc_ref[...] = (inv_rms * (gain * grad - normed * (row_dot / width))).astype(jnp.bfloat16)


def per_device(sizes, enc_states, norm_gain, kv_weight, queries, attn_cotangent, target_lengths):
    cores, parts, seqs = sizes
    rows = enc_states[0]
    tokens, feats = rows.shape
    weight = kv_weight[0]
    width = weight.shape[0]
    half = width // 2
    query, cot = queries[0, 0], attn_cotangent[0, 0]
    dec = query.shape[0]
    heads = query.shape[1] // HS
    gain = norm_gain.reshape(1, width)
    swap = [(0, 1), (1, 0)]

    def to_section(x, step):
        pairs = [
            (c * parts + i, c * parts + (i ^ section_step(c, step, parts)))
            for c in range(cores)
            for i in range(parts)
        ]
        return lax.ppermute(x, ("sec", "section"), pairs)

    def to_core(x):
        return lax.ppermute(x, "sec", swap)

    token = pl.pallas_call(
        first_kernel,
        out_shape=jax.ShapeDtypeStruct((8, 128), jnp.float32),
        out_specs=VMEM,
        compiler_params=pltpu.CompilerParams(vmem_limit_bytes=1 << 20),
        cost_estimate=pl.CostEstimate(flops=20_000_000_000, bytes_accessed=4096, transcendentals=0),
        name="first",
    )()
    flops = 2 * tokens * width * weight.shape[1]
    chunks = [rows]
    for k in range(1, parts):
        chunks.append(lax.optimization_barrier((to_section(rows, k), token))[0])
    others = [to_core(c) for c in chunks]
    att, sib, kv_grad, inv_rms = pl.pallas_call(
        functools.partial(main_kernel, parts, heads),
        out_shape=(
            jax.ShapeDtypeStruct(query.shape, jnp.bfloat16),
            jax.ShapeDtypeStruct((tokens + 8, half), jnp.bfloat16),
            jax.ShapeDtypeStruct((tokens, weight.shape[1]), jnp.bfloat16),
            jax.ShapeDtypeStruct((tokens, 1), jnp.float32),
        ),
        in_specs=[SMEM, ANY] + [VMEM] * (2 * parts + 4),
        out_specs=(ANY, VMEM, VMEM, VMEM),
        scratch_shapes=[
            pltpu.VMEM((tokens, weight.shape[1]), jnp.float32),
            pltpu.VMEM(query.shape, jnp.bfloat16),
            pltpu.SemaphoreType.DMA(()),
        ],
        compiler_params=pltpu.CompilerParams(vmem_limit_bytes=16 << 20),
        cost_estimate=pl.CostEstimate(
            flops=2 * flops, bytes_accessed=2 * weight.size, transcendentals=dec * tokens * heads
        ),
        name="main",
    )(
        target_lengths,
        token,
        *chunks,
        *others,
        gain,
        weight,
        query,
        cot,
    )
    own = pl.pallas_call(
        back_kernel,
        out_shape=jax.ShapeDtypeStruct((tokens, half), jnp.float32),
        in_specs=[VMEM, VMEM],
        out_specs=VMEM,
        compiler_params=pltpu.CompilerParams(vmem_limit_bytes=16 << 20),
        cost_estimate=pl.CostEstimate(
            flops=flops // 2, bytes_accessed=weight.size, transcendentals=0
        ),
        name="back",
    )(kv_grad, weight)
    sib_in = to_core(sib)

    kept, *big = pl.pallas_call(
        functools.partial(chip_kernel, parts),
        out_shape=(jax.ShapeDtypeStruct((tokens, feats), jnp.float32),)
        + (jax.ShapeDtypeStruct((tokens, feats), jnp.bfloat16),) * (parts - 1),
        in_specs=[VMEM] * 2,
        out_specs=(VMEM,) * parts,
        compiler_params=pltpu.CompilerParams(vmem_limit_bytes=16 << 20),
        cost_estimate=pl.CostEstimate(
            flops=2 * tokens * half, bytes_accessed=8 * tokens * half, transcendentals=0
        ),
        name="chip",
    )(own, sib_in)
    small = pl.pallas_call(
        functools.partial(gain_kernel, parts),
        out_shape=(jax.ShapeDtypeStruct((1, feats + tokens), jnp.float32),) * parts,
        in_specs=[VMEM] * (3 + 2 * parts),
        out_specs=(VMEM,) * parts,
        compiler_params=pltpu.CompilerParams(vmem_limit_bytes=16 << 20),
        cost_estimate=pl.CostEstimate(
            flops=20_000_000_000, bytes_accessed=8 * tokens * half, transcendentals=0
        ),
        name="gain",
    )(sib, sib_in, inv_rms, *chunks, kept, *big)

    big_in = [to_section(big[k - 1], k) for k in range(1, parts)]
    small_in = [small[0]] + [to_section(small[k], k) for k in range(1, parts)]
    gain_term = tree_sum([x[:, :feats] for x in small_in])
    direct = seqs <= 8 and (feats // seqs) % 128 == 0
    pieces = []
    if direct:
        piece = feats // seqs
        dp = lax.axis_index("dp")
        pieces = [lax.dynamic_slice_in_dim(gain_term, dp * piece, piece, 1)]
        for k in reversed(range(1, seqs)):
            send = lax.dynamic_slice_in_dim(gain_term, (dp ^ k) * piece, piece, 1)
            pieces.append(lax.ppermute(send, "dp", [(i, i ^ k) for i in range(seqs)]))
    enc_grad, row_dot = pl.pallas_call(
        functools.partial(last_kernel, parts, width),
        out_shape=(
            jax.ShapeDtypeStruct((tokens, feats), jnp.bfloat16),
            jax.ShapeDtypeStruct((1, tokens), jnp.float32),
        ),
        in_specs=[VMEM] * (2 * parts + 3),
        out_specs=(VMEM, VMEM),
        compiler_params=pltpu.CompilerParams(vmem_limit_bytes=8 << 20),
        cost_estimate=pl.CostEstimate(flops=20_000_000_000, bytes_accessed=4096, transcendentals=0),
        name="last",
    )(kept, *big_in, rows, inv_rms, gain, *small_in)
    if direct:
        enc_grad, pieces[0] = lax.optimization_barrier((enc_grad, pieces[0]))
        gain_grad = tree_sum(pieces)[0]
    else:
        gain_grad = lax.psum_scatter(gain_term[0], "dp", scatter_dimension=0, tiled=True)
    return (att[None, None], enc_grad[None], gain_grad, row_dot)


def solution(mesh):
    sizes = tuple(mesh.shape[a] for a in ("sec", "section", "dp"))
    placed = (
        P("dp", None, ("sec", "section")),
        P(),
        P("sec", None, "section"),
        P("sec", "dp", None, "section"),
        P("sec", "dp", None, "section"),
        P("dp"),
    )
    return jax.shard_map(
        functools.partial(per_device, sizes),
        mesh=mesh,
        in_specs=placed,
        out_specs=(
            P("sec", "dp", None, "section"),
            P("dp", None, ("sec", "section")),
            P(("sec", "section", "dp")),
            P("dp", None),
        ),
        check_vma=False,
    )
```

```python
import functools

import jax
import jax.numpy as jnp
from jax import lax
from jax.experimental import pallas as pl
from jax.experimental.pallas import tpu as pltpu
from jax.sharding import PartitionSpec as P

HS = 256
EPS = 1e-06
ROW_TERMS = 3
LAST = (((1,), (1,)), ((), ()))
FIRST = (((0,), (0,)), ((), ()))
VMEM = pl.BlockSpec(memory_space=pltpu.VMEM)
SMEM = pl.BlockSpec(memory_space=pltpu.SMEM)
ANY = pl.BlockSpec(memory_space=pl.ANY)


def tree_sum(terms):
    while len(terms) > 1:
        terms = [terms[i] + terms[i + 1] for i in range(0, len(terms), 2)]
    return terms[0]


def first_kernel(token_ref):
    token_ref[...] = jnp.zeros_like(token_ref)


def main_kernel(
    parts,
    heads,
    length_ref,
    token_ref,
    *refs,
):
    chunk_refs, refs = refs[: 2 * parts], refs[2 * parts :]
    (gain_ref, weight, query_ref, cot_ref) = refs[:4]
    (att_hbm, sib_ref, kv_grad, inv_ref, normed_ref) = refs[4:9]
    (kv, att_ref, sem) = refs[9:]
    tokens, feats = chunk_refs[0].shape
    width = weight.shape[0]
    half = width // 2
    me = lax.axis_index("sec")

    section = lax.axis_index("section")
    square = None
    for ref in chunk_refs:
        x = ref[...].astype(jnp.float32)
        x = x * x
        for i in range(0, feats, 128):
            square = x[:, i : i + 128] if square is None else square + x[:, i : i + 128]
    inv_rms = lax.rsqrt(jnp.sum(square, axis=1, keepdims=True) / width + EPS)
    inv_ref[...] = inv_rms
    for j, ref in enumerate(chunk_refs):
        owner = me if j < parts else 1 - me
        peer = section ^ (j % parts)
        cols = pl.ds(pl.multiple_of((owner * parts + peer) * feats, feats), feats)
        normed = ref[...].astype(jnp.float32) * inv_rms
        if j < parts:
            normed_ref[:, pl.ds(j * feats, feats)] = normed
        memory = (normed * gain_ref[:, cols]).astype(jnp.bfloat16)
        product = jnp.dot(memory, weight[cols, :], preferred_element_type=jnp.float32)
        if j == 0:
            kv[...] = product
        else:
            kv[...] += product

    scale = HS ** (-0.5)
    live = lax.broadcasted_iota(jnp.int32, (query_ref.shape[0], HS), 0) < length_ref[0]
    every = range(heads)
    cols = [pl.ds(h * HS, HS) for h in every]
    key_cols = [pl.ds(2 * h * HS, HS) for h in every]
    value_cols = [pl.ds((2 * h + 1) * HS, HS) for h in every]
    key_rows = [kv[:, c].astype(jnp.bfloat16) for c in key_cols]
    value_rows = [kv[:, c].astype(jnp.bfloat16) for c in value_cols]
    query = [query_ref[:, c] for c in cols]
    masked = [jnp.where(live, cot_ref[:, c], jnp.zeros((), jnp.bfloat16)) for c in cols]
    scores = [
        lax.dot_general(key_rows[h], query[h], LAST, preferred_element_type=jnp.float32) * scale
        for h in every
    ]
    back = [
        lax.dot_general(value_rows[h], masked[h], LAST, preferred_element_type=jnp.float32)
        for h in every
    ]
    exponent = [jnp.exp(x) for x in scores]
    attention = [x / jnp.sum(x, axis=0, keepdims=True) for x in exponent]
    weights_b = [x.astype(jnp.bfloat16) for x in attention]
    mean = [jnp.sum(attention[h] * back[h], axis=0, keepdims=True) for h in every]
    score_grad = [
        (attention[h] * (back[h] - mean[h]) * scale).astype(jnp.bfloat16) for h in every
    ]
    key_grad = [
        jnp.dot(score_grad[h], query[h], preferred_element_type=jnp.float32).astype(jnp.bfloat16)
        for h in every
    ]
    value_grad = [
        jnp.dot(weights_b[h], masked[h], preferred_element_type=jnp.float32).astype(jnp.bfloat16)
        for h in every
    ]
    row_part = None
    for h in every:
        kv_grad[:, key_cols[h]] = key_grad[h]
        kv_grad[:, value_cols[h]] = value_grad[h]
        here = key_grad[h].astype(jnp.float32) * kv[:, key_cols[h]]
        here = here + value_grad[h].astype(jnp.float32) * kv[:, value_cols[h]]
        row_part = here if row_part is None else row_part + here
    row_part = jnp.sum(row_part, axis=1, keepdims=True)
    for h in every:
        att_ref[:, cols[h]] = lax.dot_general(
            weights_b[h], value_rows[h], FIRST, preferred_element_type=jnp.float32
        ).astype(jnp.bfloat16)
    att_out = pltpu.make_async_copy(att_ref, att_hbm, sem)
    att_out.start()
    rest = jnp.transpose(jnp.broadcast_to(row_part, (tokens, 128)))[0:8, :]
    pieces = jnp.zeros_like(rest)
    place = lax.broadcasted_iota(jnp.int32, rest.shape, 0)
    for i in range(ROW_TERMS):
        term = rest.astype(jnp.bfloat16).astype(jnp.float32)
        pieces = jnp.where(place == i, term, pieces)
        rest = rest - term
    sib_ref[pl.ds(tokens, 8), :] = jnp.zeros((8, half), jnp.bfloat16)
    sib_ref[pl.ds(tokens, 8), pl.ds(0, 128)] = pieces.astype(jnp.bfloat16)

    grad = kv_grad[...]
    tile = half // 4
    for t in range(4):
        rows = pl.ds(pl.multiple_of((1 - me) * half + t * tile, tile), tile)
        part = lax.dot_general(weight[rows, :], grad, LAST, preferred_element_type=jnp.float32)
        sib_ref[pl.ds(0, tokens), pl.ds(t * tile, tile)] = jnp.transpose(part).astype(jnp.bfloat16)
    att_out.wait()


def back_kernel(grad_ref, weight, own_ref):
    half = own_ref.shape[1]
    me = lax.axis_index("sec")
    grad = grad_ref[...]
    tile = half // 8
    for t in range(8):
        rows = pl.ds(pl.multiple_of(me * half + t * tile, tile), tile)
        own_ref[:, pl.ds(t * tile, tile)] = jnp.transpose(
            lax.dot_general(weight[rows, :], grad, LAST, preferred_element_type=jnp.float32)
        )


def chip_kernel(parts, own_ref, sent_ref, sib_ref, normed_ref, *refs):
    kept_ref, big_refs, small_refs = refs[0], refs[1:parts], refs[parts:]
    tokens, feats = kept_ref.shape
    me, section = lax.axis_index("sec"), lax.axis_index("section")
    row = 0.0
    for ref in (sent_ref, sib_ref):
        terms = ref[pl.ds(tokens, 8), pl.ds(0, 128)].astype(jnp.float32)
        row = row + ((terms[0:1, :] + terms[1:2, :]) + terms[2:3, :])
    for k in range(parts):
        cols = pl.ds(pl.multiple_of((section ^ k) * feats, feats), feats)
        total = own_ref[:, cols] + sib_ref[pl.ds(0, tokens), cols].astype(jnp.float32)
        if k == 0:
            kept_ref[...] = total
        else:
            big_refs[k - 1][...] = total.astype(jnp.bfloat16)
        normed = normed_ref[:, pl.ds(k * feats, feats)]
        small_refs[k][:, pl.ds(0, feats)] = jnp.sum(total * normed, axis=0, keepdims=True)
        small_refs[k][:, pl.ds(feats, tokens)] = row


def last_kernel(parts, width, kept_ref, *refs):
    big_refs, (chunk_ref, inv_ref, gain_ref) = refs[: parts - 1], refs[parts - 1 : parts + 2]
    small_refs, (enc_ref, row_ref) = refs[parts + 2 : 2 * parts + 2], refs[2 * parts + 2 :]
    tokens, feats = chunk_ref.shape
    core = lax.axis_index("sec")
    rows = [ref[:, pl.ds(feats, tokens)] for ref in small_refs]
    row = tree_sum(rows)
    row_ref[...] = row
    grad = kept_ref[...]
    for ref in big_refs:
        grad = grad + ref[...].astype(jnp.float32)
    inv_rms = inv_ref[...]
    at = pl.multiple_of((core * parts + lax.axis_index("section")) * feats, feats)
    gain = gain_ref[:, pl.ds(at, feats)]
    normed = chunk_ref[...].astype(jnp.float32) * inv_rms
    row_dot = jnp.transpose(jnp.broadcast_to(row, (128, tokens)))[:, 0:1]
    enc_ref[...] = (inv_rms * (gain * grad - normed * (row_dot / width))).astype(jnp.bfloat16)


def per_device(sizes, enc_states, norm_gain, kv_weight, queries, attn_cotangent, target_lengths):
    cores, parts, seqs = sizes
    rows = enc_states[0]
    tokens, feats = rows.shape
    weight = kv_weight[0]
    width = weight.shape[0]
    half = width // 2
    query, cot = queries[0, 0], attn_cotangent[0, 0]
    dec = query.shape[0]
    heads = query.shape[1] // HS
    gain = norm_gain.reshape(1, width)
    swap = [(0, 1), (1, 0)]

    def to_section(x, step):
        pairs = [
            (c * parts + i, c * parts + (i ^ step))
            for c in range(cores)
            for i in range(parts)
        ]
        return lax.ppermute(x, ("sec", "section"), pairs)

    def to_core(x):
        return lax.ppermute(x, "sec", swap)

    token = pl.pallas_call(
        first_kernel,
        out_shape=jax.ShapeDtypeStruct((8, 128), jnp.float32),
        out_specs=VMEM,
        compiler_params=pltpu.CompilerParams(vmem_limit_bytes=1 << 20),
        cost_estimate=pl.CostEstimate(flops=20_000_000_000, bytes_accessed=4096, transcendentals=0),
        name="first",
    )()
    flops = 2 * tokens * width * weight.shape[1]
    chunks = [rows]
    for k in range(1, parts):
        chunks.append(lax.optimization_barrier((to_section(rows, k), token))[0])
    others = [to_core(c) for c in chunks]
    att, sib, kv_grad, inv_rms, normed = pl.pallas_call(
        functools.partial(main_kernel, parts, heads),
        out_shape=(
            jax.ShapeDtypeStruct(query.shape, jnp.bfloat16),
            jax.ShapeDtypeStruct((tokens + 8, half), jnp.bfloat16),
            jax.ShapeDtypeStruct((tokens, weight.shape[1]), jnp.bfloat16),
            jax.ShapeDtypeStruct((tokens, 1), jnp.float32),
            jax.ShapeDtypeStruct((tokens, half), jnp.float32),
        ),
        in_specs=[SMEM, ANY] + [VMEM] * (2 * parts + 4),
        out_specs=(ANY, VMEM, VMEM, VMEM, VMEM),
        scratch_shapes=[
            pltpu.VMEM((tokens, weight.shape[1]), jnp.float32),
            pltpu.VMEM(query.shape, jnp.bfloat16),
            pltpu.SemaphoreType.DMA(()),
        ],
        compiler_params=pltpu.CompilerParams(vmem_limit_bytes=16 << 20),
        cost_estimate=pl.CostEstimate(
            flops=2 * flops, bytes_accessed=2 * weight.size, transcendentals=dec * tokens * heads
        ),
        name="main",
    )(
        target_lengths,
        token,
        *chunks,
        *others,
        gain,
        weight,
        query,
        cot,
    )
    own = pl.pallas_call(
        back_kernel,
        out_shape=jax.ShapeDtypeStruct((tokens, half), jnp.float32),
        in_specs=[VMEM, VMEM],
        out_specs=VMEM,
        compiler_params=pltpu.CompilerParams(vmem_limit_bytes=16 << 20),
        cost_estimate=pl.CostEstimate(
            flops=flops // 2, bytes_accessed=weight.size, transcendentals=0
        ),
        name="back",
    )(kv_grad, weight)
    sib_in = to_core(sib)

    pieces = pl.pallas_call(
        functools.partial(chip_kernel, parts),
        out_shape=(jax.ShapeDtypeStruct((tokens, feats), jnp.float32),)
        + (jax.ShapeDtypeStruct((tokens, feats), jnp.bfloat16),) * (parts - 1)
        + (jax.ShapeDtypeStruct((1, feats + tokens), jnp.float32),) * parts,
        in_specs=[VMEM] * 4,
        out_specs=(VMEM,) * (2 * parts),
        compiler_params=pltpu.CompilerParams(vmem_limit_bytes=16 << 20),
        cost_estimate=pl.CostEstimate(
            flops=4 * tokens * half, bytes_accessed=12 * tokens * half, transcendentals=0
        ),
        name="chip",
    )(own, sib, sib_in, normed)
    kept, big, small = pieces[0], pieces[1:parts], pieces[parts:]
    big_in = [to_section(big[k - 1], k) for k in (parts - 1, *range(1, parts - 1))]
    small_in = [small[0]] + [to_section(small[k], k) for k in range(1, parts)]
    gain_term = tree_sum([x[:, :feats] for x in small_in])
    direct = seqs <= 8 and (feats // seqs) % 128 == 0
    pieces = []
    if direct:
        piece = feats // seqs
        dp = lax.axis_index("dp")
        pieces = [lax.dynamic_slice_in_dim(gain_term, dp * piece, piece, 1)]
        for k in reversed(range(1, seqs)):
            send = lax.dynamic_slice_in_dim(gain_term, (dp ^ k) * piece, piece, 1)
            pieces.append(lax.ppermute(send, "dp", [(i, i ^ k) for i in range(seqs)]))
    enc_grad, row_dot = pl.pallas_call(
        functools.partial(last_kernel, parts, width),
        out_shape=(
            jax.ShapeDtypeStruct((tokens, feats), jnp.bfloat16),
            jax.ShapeDtypeStruct((1, tokens), jnp.float32),
        ),
        in_specs=[VMEM] * (2 * parts + 3),
        out_specs=(VMEM, VMEM),
        compiler_params=pltpu.CompilerParams(vmem_limit_bytes=8 << 20),
        cost_estimate=pl.CostEstimate(flops=20_000_000_000, bytes_accessed=4096, transcendentals=0),
        name="last",
    )(kept, *big_in, rows, inv_rms, gain, *small_in)
    if direct:
        enc_grad, pieces[0] = lax.optimization_barrier((enc_grad, pieces[0]))
        gain_grad = tree_sum(pieces)[0]
    else:
        gain_grad = lax.psum_scatter(gain_term[0], "dp", scatter_dimension=0, tiled=True)
    return (att[None, None], enc_grad[None], gain_grad, row_dot)


def solution(mesh):
    sizes = tuple(mesh.shape[a] for a in ("sec", "section", "dp"))
    placed = (
        P("dp", None, ("sec", "section")),
        P(),
        P("sec", None, "section"),
        P("sec", "dp", None, "section"),
        P("sec", "dp", None, "section"),
        P("dp"),
    )
    return jax.shard_map(
        functools.partial(per_device, sizes),
        mesh=mesh,
        in_specs=placed,
        out_specs=(
            P("sec", "dp", None, "section"),
            P("dp", None, ("sec", "section")),
            P(("sec", "section", "dp")),
            P("dp", None),
        ),
        check_vma=False,
    )
```

```python
import functools

import jax
import jax.numpy as jnp
from jax import lax
from jax.experimental import pallas as pl
from jax.experimental.pallas import tpu as pltpu
from jax.sharding import PartitionSpec as P

HS = 256
EPS = 1e-06
ROW_TERMS = 3
LAST = (((1,), (1,)), ((), ()))
FIRST = (((0,), (0,)), ((), ()))
VMEM = pl.BlockSpec(memory_space=pltpu.VMEM)
SMEM = pl.BlockSpec(memory_space=pltpu.SMEM)
ANY = pl.BlockSpec(memory_space=pl.ANY)


def tree_sum(terms):
    while len(terms) > 1:
        terms = [terms[i] + terms[i + 1] for i in range(0, len(terms), 2)]
    return terms[0]


def first_kernel(token_ref):
    token_ref[...] = jnp.zeros_like(token_ref)


def main_kernel(
    parts,
    heads,
    length_ref,
    token_ref,
    *refs,
):
    chunk_refs, refs = refs[: 2 * parts], refs[2 * parts :]
    (gain_ref, weight, query_ref, cot_ref) = refs[:4]
    (att_hbm, sib_ref, kv_grad, inv_ref, normed_ref) = refs[4:9]
    (kv, att_ref, sem) = refs[9:]
    tokens, feats = chunk_refs[0].shape
    width = weight.shape[0]
    half = width // 2
    me = lax.axis_index("sec")

    section = lax.axis_index("section")
    square = None
    for ref in chunk_refs:
        x = ref[...].astype(jnp.float32)
        x = x * x
        for i in range(0, feats, 128):
            square = x[:, i : i + 128] if square is None else square + x[:, i : i + 128]
    inv_rms = lax.rsqrt(jnp.sum(square, axis=1, keepdims=True) / width + EPS)
    inv_ref[...] = inv_rms
    for j, ref in enumerate(chunk_refs):
        owner = me if j < parts else 1 - me
        peer = section ^ (j % parts)
        cols = pl.ds(pl.multiple_of((owner * parts + peer) * feats, feats), feats)
        normed = ref[...].astype(jnp.float32) * inv_rms
        if j < parts:
            normed_ref[:, pl.ds(j * feats, feats)] = normed
        memory = (normed * gain_ref[:, cols]).astype(jnp.bfloat16)
        product = jnp.dot(memory, weight[cols, :], preferred_element_type=jnp.float32)
        if j == 0:
            kv[...] = product
        else:
            kv[...] += product

    scale = HS ** (-0.5)
    live = lax.broadcasted_iota(jnp.int32, (query_ref.shape[0], HS), 0) < length_ref[0]
    every = range(heads)
    cols = [pl.ds(h * HS, HS) for h in every]
    key_cols = [pl.ds(2 * h * HS, HS) for h in every]
    value_cols = [pl.ds((2 * h + 1) * HS, HS) for h in every]
    key_rows = [kv[:, c].astype(jnp.bfloat16) for c in key_cols]
    value_rows = [kv[:, c].astype(jnp.bfloat16) for c in value_cols]
    query = [query_ref[:, c] for c in cols]
    masked = [jnp.where(live, cot_ref[:, c], jnp.zeros((), jnp.bfloat16)) for c in cols]
    scores = [
        lax.dot_general(key_rows[h], query[h], LAST, preferred_element_type=jnp.float32) * scale
        for h in every
    ]
    back = [
        lax.dot_general(value_rows[h], masked[h], LAST, preferred_element_type=jnp.float32)
        for h in every
    ]
    exponent = [jnp.exp(x) for x in scores]
    attention = [x / jnp.sum(x, axis=0, keepdims=True) for x in exponent]
    weights_b = [x.astype(jnp.bfloat16) for x in attention]
    mean = [jnp.sum(attention[h] * back[h], axis=0, keepdims=True) for h in every]
    score_grad = [
        (attention[h] * (back[h] - mean[h]) * scale).astype(jnp.bfloat16) for h in every
    ]
    key_grad = [
        jnp.dot(score_grad[h], query[h], preferred_element_type=jnp.float32).astype(jnp.bfloat16)
        for h in every
    ]
    value_grad = [
        jnp.dot(weights_b[h], masked[h], preferred_element_type=jnp.float32).astype(jnp.bfloat16)
        for h in every
    ]
    row_part = None
    for h in every:
        kv_grad[:, key_cols[h]] = key_grad[h]
        kv_grad[:, value_cols[h]] = value_grad[h]
        here = key_grad[h].astype(jnp.float32) * kv[:, key_cols[h]]
        here = here + value_grad[h].astype(jnp.float32) * kv[:, value_cols[h]]
        row_part = here if row_part is None else row_part + here
    row_part = jnp.sum(row_part, axis=1, keepdims=True)
    for h in every:
        att_ref[:, cols[h]] = lax.dot_general(
            weights_b[h], value_rows[h], FIRST, preferred_element_type=jnp.float32
        ).astype(jnp.bfloat16)
    att_out = pltpu.make_async_copy(att_ref, att_hbm, sem)
    att_out.start()
    rest = jnp.transpose(jnp.broadcast_to(row_part, (tokens, 128)))[0:8, :]
    pieces = jnp.zeros_like(rest)
    place = lax.broadcasted_iota(jnp.int32, rest.shape, 0)
    for i in range(ROW_TERMS):
        term = rest.astype(jnp.bfloat16).astype(jnp.float32)
        pieces = jnp.where(place == i, term, pieces)
        rest = rest - term
    sib_ref[pl.ds(tokens, 8), :] = jnp.zeros((8, half), jnp.bfloat16)
    sib_ref[pl.ds(tokens, 8), pl.ds(0, 128)] = pieces.astype(jnp.bfloat16)

    grad = kv_grad[...]
    tile = half // 4
    for t in range(4):
        rows = pl.ds(pl.multiple_of((1 - me) * half + t * tile, tile), tile)
        part = lax.dot_general(weight[rows, :], grad, LAST, preferred_element_type=jnp.float32)
        sib_ref[pl.ds(0, tokens), pl.ds(t * tile, tile)] = jnp.transpose(part).astype(jnp.bfloat16)
    att_out.wait()


def back_kernel(grad_ref, weight, own_ref):
    half = own_ref.shape[1]
    me = lax.axis_index("sec")
    grad = grad_ref[...]
    tile = half // 8
    for t in range(8):
        rows = pl.ds(pl.multiple_of(me * half + t * tile, tile), tile)
        own_ref[:, pl.ds(t * tile, tile)] = jnp.transpose(
            lax.dot_general(weight[rows, :], grad, LAST, preferred_element_type=jnp.float32)
        )


def chip_kernel(parts, own_ref, sent_ref, sib_ref, normed_ref, *refs):
    kept_ref, big_refs, small_refs = refs[0], refs[1:parts], refs[parts:]
    tokens, feats = kept_ref.shape
    me, section = lax.axis_index("sec"), lax.axis_index("section")
    row = 0.0
    for ref in (sent_ref, sib_ref):
        terms = ref[pl.ds(tokens, 8), pl.ds(0, 128)].astype(jnp.float32)
        row = row + ((terms[0:1, :] + terms[1:2, :]) + terms[2:3, :])
    for k in range(parts):
        cols = pl.ds(pl.multiple_of((section ^ k) * feats, feats), feats)
        total = own_ref[:, cols] + sib_ref[pl.ds(0, tokens), cols].astype(jnp.float32)
        if k == 0:
            kept_ref[...] = total
        else:
            big_refs[k - 1][...] = total.astype(jnp.bfloat16)
        normed = normed_ref[:, pl.ds(k * feats, feats)]
        small_refs[k][:, pl.ds(0, feats)] = jnp.sum(total * normed, axis=0, keepdims=True)
        small_refs[k][:, pl.ds(feats, tokens)] = row


def last_kernel(parts, width, kept_ref, *refs):
    big_refs, (chunk_ref, inv_ref, gain_ref) = refs[: parts - 1], refs[parts - 1 : parts + 2]
    small_refs, (enc_ref, row_ref) = refs[parts + 2 : 2 * parts + 2], refs[2 * parts + 2 :]
    tokens, feats = chunk_ref.shape
    core = lax.axis_index("sec")
    rows = [ref[:, pl.ds(feats, tokens)] for ref in small_refs]
    row = tree_sum(rows)
    row_ref[...] = row
    grad = kept_ref[...]
    for ref in big_refs:
        grad = grad + ref[...].astype(jnp.float32)
    inv_rms = inv_ref[...]
    at = pl.multiple_of((core * parts + lax.axis_index("section")) * feats, feats)
    gain = gain_ref[:, pl.ds(at, feats)]
    normed = chunk_ref[...].astype(jnp.float32) * inv_rms
    row_dot = jnp.transpose(jnp.broadcast_to(row, (128, tokens)))[:, 0:1]
    enc_ref[...] = (inv_rms * (gain * grad - normed * (row_dot / width))).astype(jnp.bfloat16)


def per_device(sizes, enc_states, norm_gain, kv_weight, queries, attn_cotangent, target_lengths):
    cores, parts, seqs = sizes
    rows = enc_states[0]
    tokens, feats = rows.shape
    weight = kv_weight[0]
    width = weight.shape[0]
    half = width // 2
    query, cot = queries[0, 0], attn_cotangent[0, 0]
    dec = query.shape[0]
    heads = query.shape[1] // HS
    gain = norm_gain.reshape(1, width)
    swap = [(0, 1), (1, 0)]

    def to_section(x, step):
        pairs = [
            (c * parts + i, c * parts + (i ^ step))
            for c in range(cores)
            for i in range(parts)
        ]
        return lax.ppermute(x, ("sec", "section"), pairs)

    def to_core(x):
        return lax.ppermute(x, "sec", swap)

    token = pl.pallas_call(
        first_kernel,
        out_shape=jax.ShapeDtypeStruct((8, 128), jnp.float32),
        out_specs=VMEM,
        compiler_params=pltpu.CompilerParams(vmem_limit_bytes=1 << 20),
        cost_estimate=pl.CostEstimate(flops=20_000_000_000, bytes_accessed=4096, transcendentals=0),
        name="first",
    )()
    flops = 2 * tokens * width * weight.shape[1]
    chunks = [rows]
    for k in range(1, parts):
        chunks.append(lax.optimization_barrier((to_section(rows, k), token))[0])
    others = [to_core(c) for c in chunks]
    att, sib, kv_grad, inv_rms, normed = pl.pallas_call(
        functools.partial(main_kernel, parts, heads),
        out_shape=(
            jax.ShapeDtypeStruct(query.shape, jnp.bfloat16),
            jax.ShapeDtypeStruct((tokens + 8, half), jnp.bfloat16),
            jax.ShapeDtypeStruct((tokens, weight.shape[1]), jnp.bfloat16),
            jax.ShapeDtypeStruct((tokens, 1), jnp.float32),
            jax.ShapeDtypeStruct((tokens, half), jnp.float32),
        ),
        in_specs=[SMEM, ANY] + [VMEM] * (2 * parts + 4),
        out_specs=(ANY, VMEM, VMEM, VMEM, VMEM),
        scratch_shapes=[
            pltpu.VMEM((tokens, weight.shape[1]), jnp.float32),
            pltpu.VMEM(query.shape, jnp.bfloat16),
            pltpu.SemaphoreType.DMA(()),
        ],
        compiler_params=pltpu.CompilerParams(vmem_limit_bytes=16 << 20),
        cost_estimate=pl.CostEstimate(
            flops=2 * flops, bytes_accessed=2 * weight.size, transcendentals=dec * tokens * heads
        ),
        name="main",
    )(
        target_lengths,
        token,
        *chunks,
        *others,
        gain,
        weight,
        query,
        cot,
    )
    own = pl.pallas_call(
        back_kernel,
        out_shape=jax.ShapeDtypeStruct((tokens, half), jnp.float32),
        in_specs=[VMEM, VMEM],
        out_specs=VMEM,
        compiler_params=pltpu.CompilerParams(vmem_limit_bytes=16 << 20),
        cost_estimate=pl.CostEstimate(
            flops=flops // 2, bytes_accessed=weight.size, transcendentals=0
        ),
        name="back",
    )(kv_grad, weight)
    sib_in = to_core(sib)

    pieces = pl.pallas_call(
        functools.partial(chip_kernel, parts),
        out_shape=(jax.ShapeDtypeStruct((tokens, feats), jnp.float32),)
        + (jax.ShapeDtypeStruct((tokens, feats), jnp.bfloat16),) * (parts - 1)
        + (jax.ShapeDtypeStruct((1, feats + tokens), jnp.float32),) * parts,
        in_specs=[VMEM] * 4,
        out_specs=(VMEM,) * (2 * parts),
        compiler_params=pltpu.CompilerParams(vmem_limit_bytes=16 << 20),
        cost_estimate=pl.CostEstimate(
            flops=4 * tokens * half, bytes_accessed=12 * tokens * half, transcendentals=0
        ),
        name="chip",
    )(own, sib, sib_in, normed)
    kept, big, small = pieces[0], pieces[1:parts], pieces[parts:]
    big_in = [to_section(big[k - 1], k) for k in (parts - 1, *range(1, parts - 1))]
    small_in = [small[0]] + [to_section(small[k], k) for k in range(1, parts)]
    gain_term = tree_sum([x[:, :feats] for x in small_in])
    direct = seqs <= 8 and (feats // seqs) % 128 == 0
    pieces = []
    if direct:
        piece = feats // seqs
        dp = lax.axis_index("dp")
        pieces = [lax.dynamic_slice_in_dim(gain_term, dp * piece, piece, 1)]
        for k in ((2, 3, 1) if seqs == 4 else range(1, seqs)):
            send = lax.dynamic_slice_in_dim(gain_term, (dp ^ k) * piece, piece, 1)
            pieces.append(lax.ppermute(send, "dp", [(i, i ^ k) for i in range(seqs)]))
    enc_grad, row_dot = pl.pallas_call(
        functools.partial(last_kernel, parts, width),
        out_shape=(
            jax.ShapeDtypeStruct((tokens, feats), jnp.bfloat16),
            jax.ShapeDtypeStruct((1, tokens), jnp.float32),
        ),
        in_specs=[VMEM] * (2 * parts + 3),
        out_specs=(VMEM, VMEM),
        compiler_params=pltpu.CompilerParams(vmem_limit_bytes=8 << 20),
        cost_estimate=pl.CostEstimate(flops=20_000_000_000, bytes_accessed=4096, transcendentals=0),
        name="last",
    )(kept, *big_in, rows, inv_rms, gain, *small_in)
    if direct:
        enc_grad, pieces[0] = lax.optimization_barrier((enc_grad, pieces[0]))
        gain_grad = tree_sum(pieces)[0]
    else:
        gain_grad = lax.psum_scatter(gain_term[0], "dp", scatter_dimension=0, tiled=True)
    return (att[None, None], enc_grad[None], gain_grad, row_dot)


def solution(mesh):
    sizes = tuple(mesh.shape[a] for a in ("sec", "section", "dp"))
    placed = (
        P("dp", None, ("sec", "section")),
        P(),
        P("sec", None, "section"),
        P("sec", "dp", None, "section"),
        P("sec", "dp", None, "section"),
        P("dp"),
    )
    return jax.shard_map(
        functools.partial(per_device, sizes),
        mesh=mesh,
        in_specs=placed,
        out_specs=(
            P("sec", "dp", None, "section"),
            P("dp", None, ("sec", "section")),
            P(("sec", "section", "dp")),
            P("dp", None),
        ),
        check_vma=False,
    )
```

```python
import functools

import jax
import jax.numpy as jnp
from jax import lax
from jax.experimental import pallas as pl
from jax.experimental.pallas import tpu as pltpu
from jax.sharding import PartitionSpec as P

HS = 256
EPS = 1e-06
ROW_TERMS = 3
LAST = (((1,), (1,)), ((), ()))
FIRST = (((0,), (0,)), ((), ()))
VMEM = pl.BlockSpec(memory_space=pltpu.VMEM)
SMEM = pl.BlockSpec(memory_space=pltpu.SMEM)
ANY = pl.BlockSpec(memory_space=pl.ANY)


def tree_sum(terms):
    while len(terms) > 1:
        terms = [terms[i] + terms[i + 1] for i in range(0, len(terms), 2)]
    return terms[0]


def first_kernel(token_ref):
    token_ref[...] = jnp.zeros_like(token_ref)


def main_kernel(
    parts,
    heads,
    length_ref,
    token_ref,
    *refs,
):
    chunk_refs, refs = refs[: 2 * parts], refs[2 * parts :]
    (gain_ref, weight, query_ref, cot_ref) = refs[:4]
    (att_hbm, sib_ref, kv_grad, inv_ref, normed_ref) = refs[4:9]
    (kv, att_ref, sem) = refs[9:]
    tokens, feats = chunk_refs[0].shape
    width = weight.shape[0]
    half = width // 2
    me = lax.axis_index("sec")

    section = lax.axis_index("section")
    square = None
    for ref in chunk_refs:
        x = ref[...].astype(jnp.float32)
        x = x * x
        for i in range(0, feats, 128):
            square = x[:, i : i + 128] if square is None else square + x[:, i : i + 128]
    inv_rms = lax.rsqrt(jnp.sum(square, axis=1, keepdims=True) / width + EPS)
    inv_ref[...] = inv_rms
    for j, ref in enumerate(chunk_refs):
        owner = me if j < parts else 1 - me
        peer = section ^ (j % parts)
        cols = pl.ds(pl.multiple_of((owner * parts + peer) * feats, feats), feats)
        normed = ref[...].astype(jnp.float32) * inv_rms
        if j < parts:
            normed_ref[:, pl.ds(j * feats, feats)] = normed
        memory = (normed * gain_ref[:, cols]).astype(jnp.bfloat16)
        product = jnp.dot(memory, weight[cols, :], preferred_element_type=jnp.float32)
        if j == 0:
            kv[...] = product
        else:
            kv[...] += product

    scale = HS ** (-0.5)
    live = lax.broadcasted_iota(jnp.int32, (query_ref.shape[0], HS), 0) < length_ref[0]
    every = range(heads)
    cols = [pl.ds(h * HS, HS) for h in every]
    key_cols = [pl.ds(2 * h * HS, HS) for h in every]
    value_cols = [pl.ds((2 * h + 1) * HS, HS) for h in every]
    key_rows = [kv[:, c].astype(jnp.bfloat16) for c in key_cols]
    value_rows = [kv[:, c].astype(jnp.bfloat16) for c in value_cols]
    query = [query_ref[:, c] for c in cols]
    masked = [jnp.where(live, cot_ref[:, c], jnp.zeros((), jnp.bfloat16)) for c in cols]
    scores = [
        lax.dot_general(key_rows[h], query[h], LAST, preferred_element_type=jnp.float32) * scale
        for h in every
    ]
    back = [
        lax.dot_general(value_rows[h], masked[h], LAST, preferred_element_type=jnp.float32)
        for h in every
    ]
    exponent = [jnp.exp(x) for x in scores]
    attention = [x / jnp.sum(x, axis=0, keepdims=True) for x in exponent]
    weights_b = [x.astype(jnp.bfloat16) for x in attention]
    mean = [jnp.sum(attention[h] * back[h], axis=0, keepdims=True) for h in every]
    score_grad = [
        (attention[h] * (back[h] - mean[h]) * scale).astype(jnp.bfloat16) for h in every
    ]
    key_grad = [
        jnp.dot(score_grad[h], query[h], preferred_element_type=jnp.float32).astype(jnp.bfloat16)
        for h in every
    ]
    value_grad = [
        jnp.dot(weights_b[h], masked[h], preferred_element_type=jnp.float32).astype(jnp.bfloat16)
        for h in every
    ]
    row_part = None
    for h in every:
        kv_grad[:, key_cols[h]] = key_grad[h]
        kv_grad[:, value_cols[h]] = value_grad[h]
        here = key_grad[h].astype(jnp.float32) * kv[:, key_cols[h]]
        here = here + value_grad[h].astype(jnp.float32) * kv[:, value_cols[h]]
        row_part = here if row_part is None else row_part + here
    row_part = jnp.sum(row_part, axis=1, keepdims=True)
    for h in every:
        att_ref[:, cols[h]] = lax.dot_general(
            weights_b[h], value_rows[h], FIRST, preferred_element_type=jnp.float32
        ).astype(jnp.bfloat16)
    att_out = pltpu.make_async_copy(att_ref, att_hbm, sem)
    att_out.start()
    rest = jnp.transpose(jnp.broadcast_to(row_part, (tokens, 128)))[0:8, :]
    pieces = jnp.zeros_like(rest)
    place = lax.broadcasted_iota(jnp.int32, rest.shape, 0)
    for i in range(ROW_TERMS):
        term = rest.astype(jnp.bfloat16).astype(jnp.float32)
        pieces = jnp.where(place == i, term, pieces)
        rest = rest - term
    sib_ref[pl.ds(tokens, 8), :] = jnp.zeros((8, half), jnp.bfloat16)
    sib_ref[pl.ds(tokens, 8), pl.ds(0, 128)] = pieces.astype(jnp.bfloat16)

    grad = kv_grad[...]
    tile = half // 8
    for t in range(8):
        rows = pl.ds(pl.multiple_of((1 - me) * half + t * tile, tile), tile)
        part = lax.dot_general(weight[rows, :], grad, LAST, preferred_element_type=jnp.float32)
        sib_ref[pl.ds(0, tokens), pl.ds(t * tile, tile)] = jnp.transpose(part).astype(jnp.bfloat16)
    att_out.wait()


def back_kernel(grad_ref, weight, own_ref):
    half = own_ref.shape[1]
    me = lax.axis_index("sec")
    grad = grad_ref[...]
    tile = half // 8
    for t in range(8):
        rows = pl.ds(pl.multiple_of(me * half + t * tile, tile), tile)
        own_ref[:, pl.ds(t * tile, tile)] = jnp.transpose(
            lax.dot_general(weight[rows, :], grad, LAST, preferred_element_type=jnp.float32)
        )


def chip_kernel(parts, own_ref, sent_ref, sib_ref, normed_ref, *refs):
    kept_ref, big_refs, small_refs = refs[0], refs[1:parts], refs[parts:]
    tokens, feats = kept_ref.shape
    me, section = lax.axis_index("sec"), lax.axis_index("section")
    row = 0.0
    for ref in (sent_ref, sib_ref):
        terms = ref[pl.ds(tokens, 8), pl.ds(0, 128)].astype(jnp.float32)
        row = row + ((terms[0:1, :] + terms[1:2, :]) + terms[2:3, :])
    for k in range(parts):
        cols = pl.ds(pl.multiple_of((section ^ k) * feats, feats), feats)
        total = own_ref[:, cols] + sib_ref[pl.ds(0, tokens), cols].astype(jnp.float32)
        if k == 0:
            kept_ref[...] = total
        else:
            big_refs[k - 1][...] = total.astype(jnp.bfloat16)
        normed = normed_ref[:, pl.ds(k * feats, feats)]
        small_refs[k][:, pl.ds(0, feats)] = jnp.sum(total * normed, axis=0, keepdims=True)
        small_refs[k][:, pl.ds(feats, tokens)] = row


def last_kernel(parts, width, kept_ref, *refs):
    big_refs, (chunk_ref, inv_ref, gain_ref) = refs[: parts - 1], refs[parts - 1 : parts + 2]
    small_refs, (enc_ref, row_ref) = refs[parts + 2 : 2 * parts + 2], refs[2 * parts + 2 :]
    tokens, feats = chunk_ref.shape
    core = lax.axis_index("sec")
    rows = [ref[:, pl.ds(feats, tokens)] for ref in small_refs]
    row = tree_sum(rows)
    row_ref[...] = row
    grad = kept_ref[...]
    for ref in big_refs:
        grad = grad + ref[...].astype(jnp.float32)
    inv_rms = inv_ref[...]
    at = pl.multiple_of((core * parts + lax.axis_index("section")) * feats, feats)
    gain = gain_ref[:, pl.ds(at, feats)]
    normed = chunk_ref[...].astype(jnp.float32) * inv_rms
    row_dot = jnp.transpose(jnp.broadcast_to(row, (128, tokens)))[:, 0:1]
    enc_ref[...] = (inv_rms * (gain * grad - normed * (row_dot / width))).astype(jnp.bfloat16)


def per_device(sizes, enc_states, norm_gain, kv_weight, queries, attn_cotangent, target_lengths):
    cores, parts, seqs = sizes
    rows = enc_states[0]
    tokens, feats = rows.shape
    weight = kv_weight[0]
    width = weight.shape[0]
    half = width // 2
    query, cot = queries[0, 0], attn_cotangent[0, 0]
    dec = query.shape[0]
    heads = query.shape[1] // HS
    gain = norm_gain.reshape(1, width)
    swap = [(0, 1), (1, 0)]

    def to_section(x, step):
        pairs = [
            (c * parts + i, c * parts + (i ^ step))
            for c in range(cores)
            for i in range(parts)
        ]
        return lax.ppermute(x, ("sec", "section"), pairs)

    def to_core(x):
        return lax.ppermute(x, "sec", swap)

    token = pl.pallas_call(
        first_kernel,
        out_shape=jax.ShapeDtypeStruct((8, 128), jnp.float32),
        out_specs=VMEM,
        compiler_params=pltpu.CompilerParams(vmem_limit_bytes=1 << 20),
        cost_estimate=pl.CostEstimate(flops=20_000_000_000, bytes_accessed=4096, transcendentals=0),
        name="first",
    )()
    flops = 2 * tokens * width * weight.shape[1]
    chunks = [rows]
    for k in range(1, parts):
        chunks.append(lax.optimization_barrier((to_section(rows, k), token))[0])
    others = [to_core(c) for c in chunks]
    att, sib, kv_grad, inv_rms, normed = pl.pallas_call(
        functools.partial(main_kernel, parts, heads),
        out_shape=(
            jax.ShapeDtypeStruct(query.shape, jnp.bfloat16),
            jax.ShapeDtypeStruct((tokens + 8, half), jnp.bfloat16),
            jax.ShapeDtypeStruct((tokens, weight.shape[1]), jnp.bfloat16),
            jax.ShapeDtypeStruct((tokens, 1), jnp.float32),
            jax.ShapeDtypeStruct((tokens, half), jnp.float32),
        ),
        in_specs=[SMEM, ANY] + [VMEM] * (2 * parts + 4),
        out_specs=(ANY, VMEM, VMEM, VMEM, VMEM),
        scratch_shapes=[
            pltpu.VMEM((tokens, weight.shape[1]), jnp.float32),
            pltpu.VMEM(query.shape, jnp.bfloat16),
            pltpu.SemaphoreType.DMA(()),
        ],
        compiler_params=pltpu.CompilerParams(vmem_limit_bytes=16 << 20),
        cost_estimate=pl.CostEstimate(
            flops=2 * flops, bytes_accessed=2 * weight.size, transcendentals=dec * tokens * heads
        ),
        name="main",
    )(
        target_lengths,
        token,
        *chunks,
        *others,
        gain,
        weight,
        query,
        cot,
    )
    own = pl.pallas_call(
        back_kernel,
        out_shape=jax.ShapeDtypeStruct((tokens, half), jnp.float32),
        in_specs=[VMEM, VMEM],
        out_specs=VMEM,
        compiler_params=pltpu.CompilerParams(vmem_limit_bytes=16 << 20),
        cost_estimate=pl.CostEstimate(
            flops=flops // 2, bytes_accessed=weight.size, transcendentals=0
        ),
        name="back",
    )(kv_grad, weight)
    sib_in = to_core(sib)

    pieces = pl.pallas_call(
        functools.partial(chip_kernel, parts),
        out_shape=(jax.ShapeDtypeStruct((tokens, feats), jnp.float32),)
        + (jax.ShapeDtypeStruct((tokens, feats), jnp.bfloat16),) * (parts - 1)
        + (jax.ShapeDtypeStruct((1, feats + tokens), jnp.float32),) * parts,
        in_specs=[VMEM] * 4,
        out_specs=(VMEM,) * (2 * parts),
        compiler_params=pltpu.CompilerParams(vmem_limit_bytes=16 << 20),
        cost_estimate=pl.CostEstimate(
            flops=4 * tokens * half, bytes_accessed=12 * tokens * half, transcendentals=0
        ),
        name="chip",
    )(own, sib, sib_in, normed)
    kept, big, small = pieces[0], pieces[1:parts], pieces[parts:]
    big_in = [to_section(big[k - 1], k) for k in (parts - 1, *range(1, parts - 1))]
    small_in = [small[0]] + [to_section(small[k], k) for k in range(1, parts)]
    gain_term = tree_sum([x[:, :feats] for x in small_in])
    direct = seqs <= 8 and (feats // seqs) % 128 == 0
    pieces = []
    if direct:
        piece = feats // seqs
        dp = lax.axis_index("dp")
        pieces = [lax.dynamic_slice_in_dim(gain_term, dp * piece, piece, 1)]
        for k in reversed(range(1, seqs)):
            send = lax.dynamic_slice_in_dim(gain_term, (dp ^ k) * piece, piece, 1)
            pieces.append(lax.ppermute(send, "dp", [(i, i ^ k) for i in range(seqs)]))
    enc_grad, row_dot = pl.pallas_call(
        functools.partial(last_kernel, parts, width),
        out_shape=(
            jax.ShapeDtypeStruct((tokens, feats), jnp.bfloat16),
            jax.ShapeDtypeStruct((1, tokens), jnp.float32),
        ),
        in_specs=[VMEM] * (2 * parts + 3),
        out_specs=(VMEM, VMEM),
        compiler_params=pltpu.CompilerParams(vmem_limit_bytes=8 << 20),
        cost_estimate=pl.CostEstimate(flops=20_000_000_000, bytes_accessed=4096, transcendentals=0),
        name="last",
    )(kept, *big_in, rows, inv_rms, gain, *small_in)
    if direct:
        enc_grad, pieces[0] = lax.optimization_barrier((enc_grad, pieces[0]))
        gain_grad = tree_sum(pieces)[0]
    else:
        gain_grad = lax.psum_scatter(gain_term[0], "dp", scatter_dimension=0, tiled=True)
    return (att[None, None], enc_grad[None], gain_grad, row_dot)


def solution(mesh):
    sizes = tuple(mesh.shape[a] for a in ("sec", "section", "dp"))
    placed = (
        P("dp", None, ("sec", "section")),
        P(),
        P("sec", None, "section"),
        P("sec", "dp", None, "section"),
        P("sec", "dp", None, "section"),
        P("dp"),
    )
    return jax.shard_map(
        functools.partial(per_device, sizes),
        mesh=mesh,
        in_specs=placed,
        out_specs=(
            P("sec", "dp", None, "section"),
            P("dp", None, ("sec", "section")),
            P(("sec", "section", "dp")),
            P("dp", None),
        ),
        check_vma=False,
    )
```
